256 devices in a mesh: cfg: 2 (over z_hi), seq: 16 (over z_lo, y), dp: 8 (over x, core).
Axes of the slice: x: 4, y: 4, z: 8 (z_hi: 2, z_lo: 4; z = z_hi * 4 + z_lo), core: 2. Of those that a mesh axis runs over, the one named last changes fastest.
Arguments:
- teacher_query: bfloat16 [2, 2, 8, 2048, 2048], P('cfg', None, 'dp', 'seq'), may hold values from -6 to 6
- teacher_key: bfloat16 [2, 2, 8, 2048, 2048], P('cfg', None, 'dp', 'seq'), may hold values from -6 to 6
- teacher_value: bfloat16 [2, 2, 8, 2048, 2048], P('cfg', None, 'dp', 'seq'), may hold values from -6 to 6
- hidden: bfloat16 [2, 8, 2048, 3072], P('cfg', 'dp', 'seq'), may hold values from -6 to 6
- adapter_down_weight: bfloat16 [3, 3072, 128], replicated, may hold values from -0.109375 to 0.109375
- adapter_up_weight: bfloat16 [3, 128, 2048], replicated, may hold values from -0.5 to 0.5
- guidance_index: int32 [2, 8], P(None, 'dp'), may hold values from 0 to 7
- timestep_index: int32 [2, 8], P(None, 'dp'), may hold values from 0 to 999
Outputs:
- student_out: bfloat16 [2, 8, 2048, 2048], P('cfg', 'dp', 'seq')
- grad_down: float32 [3, 3072, 128], P(None, ('cfg', 'seq', 'dp'))
- grad_up: float32 [3, 128, 2048], P(None, ('cfg', 'dp'), 'seq')
The draws below stay inside these ranges and needn't reach their ends.
All inputs are finite; a program needn't handle non-finite values.
Results may differ from the reference program's by a relative error of at most 0.02.
The reference program's roundings to bfloat16 on the way count: a program that leaves them out, or rounds other values in their place, can miss the bound.
Values may be sent and summed in bfloat16 or wider, within the bound.
No kernel may reach another device: no remote copies, remote signals or barrier semaphores. Data moves between devices by JAX's collectives and lax.ppermute only.
A program may use at most 128 MiB of HBM per device.

```python
import math
import jax
import jax.numpy as jnp
from jax import lax

MODEL_WIDTH = 3072
HEADS = 16
HDIM = 128
ADAPTER_RANK = 128
GUIDES = 8
TSTEPS = 1000
ALL_HEADS_WIDTH = 2048
TOKENS = 2048
N_DP = 8


def field_shape():
    return (2, 2, N_DP, TOKENS, HEADS * HDIM)


def draw_teacher_query(key, part):
    field = 2.7 * jax.random.truncated_normal(jax.random.fold_in(key, 11), -2.2, 2.2, field_shape(), jnp.float32)
    return field.astype(jnp.bfloat16)


def draw_teacher_key(key, part):
    field = 2.7 * jax.random.truncated_normal(jax.random.fold_in(key, 23), -2.2, 2.2, field_shape(), jnp.float32)
    return field.astype(jnp.bfloat16)


def place_ends(entries, own_key, least, largest):
    longest = entries.shape.index(max(entries.shape))
    spots = []
    for shift in (0, 1):
        where = [jax.random.randint(jax.random.fold_in(own_key, axis), (), 0, length) for axis, length in enumerate(entries.shape)]
        where[longest] = (where[longest] + shift) % entries.shape[longest]
        spots.append(tuple(where))
    return entries.at[spots[0]].set(least).at[spots[1]].set(largest)


def with_spikes(values, own_key, source, target, parts, factor):
    owner, partner = [(jnp.arange(values.shape[dim]) // (values.shape[dim] // parts)).reshape([-1 if axis == dim else 1 for axis in range(values.ndim)]) for dim in (source, target)]
    chosen = jax.random.permutation(own_key, parts)[partner]
    strong = (owner == chosen) | (owner == (partner + parts // 2) % parts)
    return jnp.where(strong, factor * values, values)


def block_scale(rng, shape, split, low, high):
    gain = 1.0
    for dim, blocks in split:
        draws = jax.random.uniform(jax.random.fold_in(jax.random.fold_in(rng, 6), dim), (blocks,), jnp.float32, low / len(split), high / len(split))
        gain = gain * jnp.repeat(jnp.exp(draws), shape[dim] // blocks).reshape((-1,) + (1,) * (len(shape) - 1 - dim))
    return gain


def noise(rng, shape, width, most, shards=(), held_as=jnp.bfloat16):
    result = jax.random.normal(rng, shape, jnp.float32) * width
    if len(shards) > 0:
        result = block_scale(rng, shape, shards, -0.22, 0.18) * result
    return jnp.clip(result, min=-most, max=most).astype(held_as)


def noise_with(own_key, shape, spread, bound, cuts, heavy, dtype=jnp.bfloat16):
    values = spread * jax.random.normal(own_key, shape, jnp.float32)
    if cuts:
        values = values * block_scale(own_key, shape, cuts, -0.22, 0.18)
    return jnp.clip(with_spikes(values, jax.random.fold_in(own_key, 3), *heavy), -bound, bound).astype(dtype)


def setup_inputs(seed: int = 0) -> dict:
    streams_of = jax.random.split(jax.random.key(seed), 9)
    return {
        "teacher_query": draw_teacher_query(jax.random.fold_in(streams_of[8], 71), 0),
        "teacher_key": draw_teacher_key(jax.random.fold_in(streams_of[8], 71), 0),
        "teacher_value": noise(streams_of[2], (2, 2, N_DP, TOKENS, ALL_HEADS_WIDTH), 1.0, 6.0, ((0, 2), (2, 8), (3, 16))),
        "hidden": noise_with(streams_of[3], (2, N_DP, TOKENS, MODEL_WIDTH), 1.0, 6.0, ((0, 2), (1, 8), (2, 16)), (2, 3, 16, 2.0)),
        "adapter_down_weight": noise(streams_of[4], (3, MODEL_WIDTH, ADAPTER_RANK), MODEL_WIDTH ** -0.5, 0.109375),
        "adapter_up_weight": noise(streams_of[5], (3, ADAPTER_RANK, ALL_HEADS_WIDTH), ADAPTER_RANK ** -0.5, 0.5),
        "guidance_index": place_ends(jax.random.randint(streams_of[6], (2, N_DP), 0, GUIDES), jax.random.fold_in(streams_of[6], 1), 0, GUIDES - 1).astype(jnp.int32),
        "timestep_index": place_ends(jax.random.randint(streams_of[7], (2, N_DP), 0, TSTEPS), jax.random.fold_in(streams_of[7], 1), 0, TSTEPS - 1).astype(jnp.int32),
    }


def head_probs(query_head, key_head):
    scores = jnp.dot(query_head, key_head.T, preferred_element_type=jnp.float32) * HDIM ** (-0.5)
    highest = lax.optimization_barrier(jnp.max(scores, axis=-1, keepdims=True))
    raised = jnp.exp(scores - highest)
    return raised / lax.optimization_barrier(jnp.sum(raised, axis=-1, keepdims=True))

def to_heads(array):
    return array.reshape(array.shape[0], HEADS, HDIM).transpose(1, 0, 2)

def from_heads(array):
    return array.transpose(1, 0, 2).reshape(array.shape[1], HEADS * HDIM)

def attend(queries, keys, values):

    def per_head(triple):
        query_head, key_head, value_head = triple
        weights = head_probs(query_head, key_head).astype(jnp.bfloat16)
        return jnp.dot(weights, value_head, preferred_element_type=jnp.float32)
    return from_heads(lax.map(per_head, (to_heads(queries), to_heads(keys), to_heads(values))))

def attend_back(queries, keys, values, upstream):
    factor = HDIM ** (-0.5)

    def per_head(group):
        query_head, key_head, value_head, upstream_head = group
        probability = head_probs(query_head, key_head)
        weights = probability.astype(jnp.bfloat16)
        value_grad = jnp.dot(weights.T, upstream_head, preferred_element_type=jnp.float32)
        prob_grad = jnp.dot(upstream_head, value_head.T, preferred_element_type=jnp.float32)
        center = lax.optimization_barrier(jnp.sum(probability * prob_grad, axis=-1, keepdims=True))
        score_grad = (probability * (prob_grad - center)).astype(jnp.bfloat16)
        query_grad = jnp.dot(score_grad, key_head, preferred_element_type=jnp.float32) * factor
        key_grad = jnp.dot(score_grad.T, query_head, preferred_element_type=jnp.float32) * factor
        return (query_grad.astype(jnp.bfloat16), key_grad.astype(jnp.bfloat16), value_grad.astype(jnp.bfloat16))
    results = lax.map(per_head, (to_heads(queries), to_heads(keys), to_heads(values), to_heads(upstream)))
    return tuple((from_heads(stack_member) for stack_member in results))

def flatten(array):
    return array.reshape(-1, TOKENS, ALL_HEADS_WIDTH)

def reference(teacher_query, teacher_key, teacher_value, hidden, adapter_down_weight, adapter_up_weight, guidance_index, timestep_index):
    teacher_out = lax.map(lambda triple: attend(*triple).astype(jnp.bfloat16), (flatten(teacher_query), flatten(teacher_key), flatten(teacher_value)))
    teacher_out = teacher_out.reshape(2, 2, N_DP, TOKENS, ALL_HEADS_WIDTH).astype(jnp.float32)
    guide_scale = 1.0 + 0.5 * guidance_index.astype(jnp.float32)
    time_frac = (timestep_index.astype(jnp.float32) + 0.5) / TSTEPS
    target = teacher_out[1] + guide_scale[:, :, None, None] * (teacher_out[0] - teacher_out[1])
    rank_index = jnp.arange(1, ADAPTER_RANK + 1).astype(jnp.float32)
    feature_modulation = 1.0 + 0.5 * jnp.cos(math.pi * rank_index * time_frac[:, :, None] + 0.25 * rank_index * guide_scale[:, :, None])
    hidden_full_width = hidden.astype(jnp.float32)
    rank_projected = (jnp.einsum('eyog,mgf->meyof', hidden_full_width, adapter_down_weight.astype(jnp.float32)) * feature_modulation[None, :, :, None, :]).astype(jnp.bfloat16)
    up_full_width = adapter_up_weight.astype(jnp.float32)
    frozen = (teacher_query[0], teacher_key[0], teacher_value[0])
    student = []
    for stack_member in range(3):
        adapted_output = jnp.einsum('citr,rh->cith', rank_projected[stack_member].astype(jnp.float32), up_full_width[stack_member])
        student.append(flatten((frozen[stack_member].astype(jnp.float32) + adapted_output).astype(jnp.bfloat16)))
    student = tuple(student)
    student_flat = lax.map(lambda triple: attend(*triple).astype(jnp.bfloat16), student)
    student_out = student_flat.reshape(2, N_DP, TOKENS, ALL_HEADS_WIDTH)
    upstream = ((student_out.astype(jnp.float32) - target) * (1.0 / math.sqrt(2 * N_DP * TOKENS))).astype(jnp.bfloat16)
    grads = lax.map(lambda group: attend_back(*group), student + (flatten(upstream),))
    gradient_stack = jnp.stack(grads).astype(jnp.float32).reshape(3, 2, N_DP, TOKENS, ALL_HEADS_WIDTH)
    grad_up = jnp.einsum('kcitr,kcith->krh', rank_projected.astype(jnp.float32), gradient_stack)
    rank_backward = jnp.einsum('kcith,krh->kcitr', gradient_stack, up_full_width)
    low_grad = (rank_backward * feature_modulation[None, :, :, None, :]).astype(jnp.bfloat16)
    grad_down = jnp.einsum('citd,kcitr->kdr', hidden_full_width, low_grad.astype(jnp.float32))
    return (student_out, grad_down, grad_up)
```

```python
import functools
import math

import jax
import jax.numpy as jnp
from jax import lax
from jax.experimental import pallas as pl
from jax.experimental.pallas import tpu as pltpu
from jax.sharding import Mesh
from jax.sharding import PartitionSpec as P

HDIM = 128
RANK = 128
TSTEPS = 1000
FACTOR = HDIM ** (-0.5)
LOG2E = math.log2(math.e)
SCALE2 = FACTOR * LOG2E
BF = jnp.bfloat16
F32 = jnp.float32
NT = (((1,), (1,)), ((), ()))
TN = (((0,), (0,)), ((), ()))
MIB = 1 << 20


def dot(a, b, dims=(((1,), (0,)), ((), ()))):
    return lax.dot_general(a, b, dims, preferred_element_type=F32)


def exchange(value, axes):
    return lax.all_to_all(value, axes, split_axis=0, concat_axis=0, tiled=True)


def copies_from_all(value, axis):
    peers = lax.axis_size(axis)
    return exchange(jnp.broadcast_to(value[None], (peers, *value.shape)), axis)


def summed_blocks(value, axes):
    return exchange(value, axes).astype(F32).sum(axis=0)


def pack_kernel(q_ref, k_ref, v_ref, out_ref):
    heads = out_ref.shape[0]
    for part, ref in enumerate((q_ref, k_ref, v_ref)):
        for head in range(heads):
            out_ref[head, part] = ref[0, :, head * HDIM : (head + 1) * HDIM]


def packed_by_head(q, k, v):
    halves, rows, columns = q.shape
    heads = columns // HDIM
    spec = pl.BlockSpec((1, rows, columns), lambda i: (i, 0, 0))
    return pl.pallas_call(
        pack_kernel,
        grid=(halves,),
        in_specs=[spec] * 3,
        out_specs=pl.BlockSpec((heads, 3, rows, HDIM), lambda i: (i, 0, 0, 0)),
        out_shape=jax.ShapeDtypeStruct((halves * heads, 3, rows, HDIM), q.dtype),
        cost_estimate=pl.CostEstimate(flops=0, transcendentals=0, bytes_accessed=12 * q.size),
        name="pack_heads",
    )(q, k, v)


def softmax_rows(query, key):
    scores = dot(query, key, NT)
    highest = jnp.max(scores, axis=-1, keepdims=True)
    raised = jnp.exp2((scores - highest) * SCALE2)
    total = jnp.sum(raised, axis=-1, keepdims=True)
    return raised.astype(BF), highest, total


def forward_kernel(
    scale_ref, heads_ref, low_ref, up_ref, inv_ref, out_ref, upstream_ref, student_ref, stats_ref, keys_ref
):
    pass_tok, rows = heads_ref.shape[1], heads_ref.shape[3]
    tokens = pass_tok * rows
    n_slow, n_fast = low_ref.shape[1], low_ref.shape[0]
    scale = scale_ref[0]
    inverse = inv_ref[0]

    for part in range(3):
        up = up_ref[part]
        for block in range(pass_tok):
            slow, fast = block // n_fast, block % n_fast
            adapted = dot(low_ref[fast, slow, :, part * RANK : (part + 1) * RANK], up)
            frozen = heads_ref[0, block, part].astype(F32)
            student_ref[part, block * rows : (block + 1) * rows] = (frozen + adapted).astype(BF)
            for one in range(2):
                keys_ref[one, part, block * rows : (block + 1) * rows] = heads_ref[one, block, part]

    step_rows = 256

    def one_block(step, carry):
        here = pl.ds(pl.multiple_of(step * step_rows, step_rows), step_rows)
        outs = []
        for one in range(2):
            raised, _, total = softmax_rows(keys_ref[one, 0, here], keys_ref[one, 1])
            attended = dot(raised, keys_ref[one, 2]) / total
            outs.append(attended.astype(BF).astype(F32))
        raised, highest, total = softmax_rows(student_ref[0, here], student_ref[1])
        attended = dot(raised, student_ref[2]) / total
        rounded = attended.astype(BF)
        out_ref[here] = rounded
        target = outs[1] + scale * (outs[0] - outs[1])
        upstream = ((rounded.astype(F32) - target) * inverse).astype(BF)
        upstream_ref[here] = upstream
        level = highest * SCALE2 + jnp.log2(total)
        center = jnp.sum(attended * upstream.astype(F32), axis=-1, keepdims=True)
        stats_ref[0:1, here] = jnp.transpose(jnp.broadcast_to(level, (step_rows, HDIM)))[0:1]
        stats_ref[1:2, here] = jnp.transpose(jnp.broadcast_to(center, (step_rows, HDIM)))[0:1]
        return carry

    stats_ref[...] = jnp.zeros_like(stats_ref)
    lax.fori_loop(0, tokens // step_rows, one_block, 0)


def forward(scale, heads, low, up, inverse):
    tokens = heads.shape[1] * heads.shape[3]
    vmem = pl.BlockSpec(memory_space=pltpu.VMEM)
    smem = pl.BlockSpec(memory_space=pltpu.SMEM)
    return pl.pallas_call(
        forward_kernel,
        in_specs=[smem, vmem, vmem, vmem, smem],
        out_specs=[vmem] * 4,
        out_shape=[
            jax.ShapeDtypeStruct((tokens, HDIM), BF),
            jax.ShapeDtypeStruct((tokens, HDIM), BF),
            jax.ShapeDtypeStruct((3, tokens, HDIM), BF),
            jax.ShapeDtypeStruct((8, tokens), F32),
        ],
        scratch_shapes=[pltpu.VMEM((2, 3, tokens, HDIM), BF)],
        cost_estimate=pl.CostEstimate(
            flops=12 * tokens * tokens * HDIM,
            transcendentals=3 * tokens * tokens,
            bytes_accessed=8 * MIB,
        ),
        compiler_params=pltpu.CompilerParams(vmem_limit_bytes=56 * MIB),
        name="attention_forward",
    )(scale, heads, low, up, inverse)


def backward_kernel(
    student_ref, upstream_ref, stats_ref, low_ref, up_ref, back_ref, grad_up_ref, dq_ref, dk_ref, dv_ref
):
    tokens = student_ref.shape[1]
    n_fast, n_slow, rows, _ = low_ref.shape
    step_rows = 256
    dk_ref[...] = jnp.zeros_like(dk_ref)
    dv_ref[...] = jnp.zeros_like(dv_ref)

    def one_block(step, carry):
        here = pl.ds(pl.multiple_of(step * step_rows, step_rows), step_rows)
        query = student_ref[0, here]
        upstream = upstream_ref[here]
        key = student_ref[1]
        level = stats_ref[0:1, here]
        center = stats_ref[1:2, here]
        prob = jnp.exp2(dot(key, query, NT) * SCALE2 - level)
        dv_ref[...] += dot(prob.astype(BF), upstream)
        dprob = dot(student_ref[2], upstream, NT)
        dscore = (prob * (dprob - center)).astype(BF)
        dk_ref[...] += dot(dscore, query)
        dq_ref[here] = dot(dscore, key, TN)
        return carry

    lax.fori_loop(0, tokens // step_rows, one_block, 0)
    for part, (ref, factor) in enumerate(((dq_ref, FACTOR), (dk_ref, FACTOR), (dv_ref, 1.0))):
        up = up_ref[part]
        total = jnp.zeros((RANK, HDIM), F32)
        for slow in range(n_slow):
            for fast in range(n_fast):
                first = (slow * n_fast + fast) * rows
                grad = (ref[first : first + rows] * factor).astype(BF)
                columns = slice(part * RANK, (part + 1) * RANK)
                back_ref[fast, slow, :, columns] = dot(grad, up, NT).astype(BF)
                total += dot(low_ref[fast, slow, :, columns], grad, TN)
        grad_up_ref[part] = total.astype(BF)


def backward(student, upstream, stats, low, up):
    tokens = student.shape[1]
    vmem = pl.BlockSpec(memory_space=pltpu.VMEM)
    return pl.pallas_call(
        backward_kernel,
        in_specs=[vmem] * 5,
        out_specs=[vmem] * 2,
        out_shape=[
            jax.ShapeDtypeStruct(low.shape, BF),
            jax.ShapeDtypeStruct((3, RANK, HDIM), BF),
        ],
        scratch_shapes=[pltpu.VMEM((tokens, HDIM), F32)] * 3,
        cost_estimate=pl.CostEstimate(
            flops=10 * tokens * tokens * HDIM,
            transcendentals=tokens * tokens,
            bytes_accessed=6 * MIB,
        ),
        compiler_params=pltpu.CompilerParams(vmem_limit_bytes=56 * MIB),
        name="attention_backward",
    )(student, upstream, stats, low, up)


def body(
    teacher_query,
    teacher_key,
    teacher_value,
    hidden,
    adapter_down_weight,
    adapter_up_weight,
    guidance_index,
    timestep_index,
):
    n_cfg, n_slow, n_fast = (lax.axis_size(a) for a in ("cfg", "z", "y"))
    n_x, n_core = (lax.axis_size(a) for a in ("x", "core"))
    cfg_index = lax.axis_index("cfg")
    seq_index = lax.axis_index(("z", "y"))
    features = hidden[0, 0]
    rows, width = features.shape
    tokens = rows * n_slow * n_fast
    total_rows = n_cfg * n_x * n_core * tokens

    packed = packed_by_head(teacher_query[0, :, 0], teacher_key[0, :, 0], teacher_value[0, :, 0])
    heads = exchange(packed, ("cfg", "z", "y"))
    heads = heads.reshape(n_cfg, n_slow * n_fast, 3, rows, HDIM)

    scale = 1.0 + 0.5 * lax.dynamic_slice(guidance_index[:, 0], (cfg_index,), (1,)).astype(F32)
    time = (lax.dynamic_slice(timestep_index[:, 0], (cfg_index,), (1,)).astype(F32) + 0.5) / TSTEPS
    rank_index = jnp.arange(1, RANK + 1).astype(F32)
    modulation = 1.0 + 0.5 * jnp.cos(math.pi * rank_index * time + 0.25 * rank_index * scale)

    low = jnp.einsum("cl,elj->cej", features, adapter_down_weight, preferred_element_type=F32)
    low = (low * modulation).astype(BF).reshape(rows, 3 * RANK)
    low_all = copies_from_all(copies_from_all(low, "z"), "y")

    groups = n_cfg * n_slow
    part_cols = width // (groups * n_fast)
    spread = jnp.moveaxis(features.reshape(rows, groups, n_fast, part_cols), 2, 0)
    columns = exchange(spread.reshape(n_fast, rows, groups * part_cols), "y")
    columns = columns.reshape(n_fast * rows, groups * part_cols)

    up = lax.dynamic_slice_in_dim(adapter_up_weight, seq_index * HDIM, HDIM, 2)
    inverse = jnp.full((1,), 1.0 / math.sqrt(total_rows), F32)
    out, upstream, student, stats = forward(scale, heads, low_all, up, inverse)
    tokens_out = exchange(out.reshape(n_slow * n_fast, rows, HDIM), ("z", "y"))
    student_out = jnp.moveaxis(tokens_out, 0, 1).reshape(rows, -1)

    back, up_partial = backward(student, upstream, stats, low_all, up)
    back = summed_blocks(back, "y").astype(BF)
    back = summed_blocks(back, "z")
    low_grad = (back.reshape(rows, 3, RANK) * modulation).astype(BF).reshape(rows, 3 * RANK)
    low_grads = copies_from_all(low_grad, "y").reshape(n_fast * rows, 3 * RANK)
    down = dot(columns, low_grads, TN).astype(BF)
    peers = groups * n_x * n_core
    down = summed_blocks(down.reshape(peers, -1, 3 * RANK), ("cfg", "z", "x", "core"))
    grad_down = jnp.moveaxis(down.reshape(-1, 3, RANK), 1, 0)

    owners = n_cfg * n_x * n_core
    up_blocks = jnp.moveaxis(up_partial.reshape(3, owners, RANK // owners, HDIM), 1, 0)
    grad_up = summed_blocks(up_blocks, ("cfg", "x", "core"))
    return student_out[None, None], grad_down, grad_up


def solution(mesh):
    sizes = {"cfg": 2, "z": 4, "y": 4, "x": 4, "core": 2}
    mesh = Mesh(mesh.devices.reshape(tuple(sizes.values())), tuple(sizes))
    seq, dp = ("z", "y"), ("x", "core")
    teacher = P("cfg", None, dp, seq, None)
    return jax.shard_map(
        body,
        mesh=mesh,
        in_specs=(
            teacher,
            teacher,
            teacher,
            P("cfg", dp, seq, None),
            P(),
            P(),
            P(None, dp),
            P(None, dp),
        ),
        out_specs=(
            P("cfg", dp, seq, None),
            P(None, ("cfg", *seq, *dp), None),
            P(None, ("cfg", *dp), seq),
        ),
        check_vma=False,
    )
```

```python
import functools
import math

import jax
import jax.numpy as jnp
from jax import lax
from jax.experimental import pallas as pl
from jax.experimental.pallas import tpu as pltpu
from jax.sharding import Mesh
from jax.sharding import PartitionSpec as P

HDIM = 128
RANK = 128
TSTEPS = 1000
FACTOR = HDIM ** (-0.5)
LOG2E = math.log2(math.e)
SCALE2 = FACTOR * LOG2E
BF = jnp.bfloat16
F32 = jnp.float32
NT = (((1,), (1,)), ((), ()))
TN = (((0,), (0,)), ((), ()))
MIB = 1 << 20


def dot(a, b, dims=(((1,), (0,)), ((), ()))):
    return lax.dot_general(a, b, dims, preferred_element_type=F32)


def exchange(value, axes):
    return lax.all_to_all(value, axes, split_axis=0, concat_axis=0, tiled=True)


def shifted(value, axis, distance):
    size = lax.axis_size(axis)
    return lax.ppermute(value, axis, [(i, (i + distance) % size) for i in range(size)])


def from_each(value, axis):
    return [value] + [shifted(value, axis, d) for d in range(1, lax.axis_size(axis))]


def summed_parts(parts, axis):
    total = parts[0].astype(F32)
    for d in range(1, lax.axis_size(axis)):
        total = total + shifted(parts[d].astype(BF), axis, d).astype(F32)
    return total


def parts_ahead(value, axis, dim):
    size, here = lax.axis_size(axis), lax.axis_index(axis)
    return [
        lax.dynamic_index_in_dim(value, (here + d) % size, dim, keepdims=False)
        for d in range(size)
    ]


def reduced(value, axes):
    for axis in axes:
        value = summed_parts(parts_ahead(value, axis, 0), axis)
    return value


def pack_kernel(q_ref, k_ref, v_ref, out_ref):
    heads = out_ref.shape[0]
    for part, ref in enumerate((q_ref, k_ref, v_ref)):
        for head in range(heads):
            out_ref[head, part] = ref[0, :, head * HDIM : (head + 1) * HDIM]


def packed_by_head(q, k, v):
    halves, rows, columns = q.shape
    heads = columns // HDIM
    spec = pl.BlockSpec((1, rows, columns), lambda i: (i, 0, 0))
    return pl.pallas_call(
        pack_kernel,
        grid=(halves,),
        in_specs=[spec] * 3,
        out_specs=pl.BlockSpec((heads, 3, rows, HDIM), lambda i: (i, 0, 0, 0)),
        out_shape=jax.ShapeDtypeStruct((halves * heads, 3, rows, HDIM), q.dtype),
        cost_estimate=pl.CostEstimate(flops=0, transcendentals=0, bytes_accessed=12 * q.size),
        name="pack_heads",
    )(q, k, v)


def softmax_rows(query, key):
    scores = dot(query, key, NT)
    highest = jnp.max(scores, axis=-1, keepdims=True)
    raised = jnp.exp2((scores - highest) * SCALE2)
    total = jnp.sum(raised, axis=-1, keepdims=True)
    return raised.astype(BF), highest, total


def forward_kernel(
    place_ref, scale_ref, inv_ref, heads_ref, up_ref, *refs
):
    low_refs, (out_ref, upstream_ref, student_ref, stats_ref, keys_ref) = refs[:-5], refs[-5:]
    pass_tok, rows = heads_ref.shape[1], heads_ref.shape[3]
    tokens = pass_tok * rows
    n_fast, n_slow = len(low_refs), low_refs[0].shape[0]
    here_slow, here_fast = place_ref[0], place_ref[1]
    scale = scale_ref[0]
    inverse = inv_ref[0]

    for part in range(3):
        up = up_ref[part]
        for block in range(pass_tok):
            for one in range(2):
                keys_ref[one, part, block * rows : (block + 1) * rows] = heads_ref[one, block, part]
        for fast in range(n_fast):
            for slow in range(n_slow):
                block = lax.rem(here_slow - slow + n_slow, n_slow) * n_fast + lax.rem(
                    here_fast - fast + n_fast, n_fast
                )
                columns = slice(part * RANK, (part + 1) * RANK)
                adapted = dot(low_refs[fast][slow, :, columns], up)
                frozen = heads_ref[0, block, part].astype(F32)
                where = pl.ds(pl.multiple_of(block * rows, rows), rows)
                student_ref[part, where] = (frozen + adapted).astype(BF)

    step_rows = 256

    def one_block(step, carry):
        here = pl.ds(pl.multiple_of(step * step_rows, step_rows), step_rows)
        outs = []
        for one in range(2):
            raised, _, total = softmax_rows(keys_ref[one, 0, here], keys_ref[one, 1])
            attended = dot(raised, keys_ref[one, 2]) / total
            outs.append(attended.astype(BF).astype(F32))
        raised, highest, total = softmax_rows(student_ref[0, here], student_ref[1])
        attended = dot(raised, student_ref[2]) / total
        rounded = attended.astype(BF)
        out_ref[here] = rounded
        target = outs[1] + scale * (outs[0] - outs[1])
        upstream = ((rounded.astype(F32) - target) * inverse).astype(BF)
        upstream_ref[here] = upstream
        level = highest * SCALE2 + jnp.log2(total)
        center = jnp.sum(attended * upstream.astype(F32), axis=-1, keepdims=True)
        stats_ref[0:1, here] = jnp.transpose(jnp.broadcast_to(level, (step_rows, HDIM)))[0:1]
        stats_ref[1:2, here] = jnp.transpose(jnp.broadcast_to(center, (step_rows, HDIM)))[0:1]
        return carry

    stats_ref[...] = jnp.zeros_like(stats_ref)
    lax.fori_loop(0, tokens // step_rows, one_block, 0)


def forward(place, scale, inverse, heads, up, low):
    tokens = heads.shape[1] * heads.shape[3]
    vmem = pl.BlockSpec(memory_space=pltpu.VMEM)
    smem = pl.BlockSpec(memory_space=pltpu.SMEM)
    return pl.pallas_call(
        forward_kernel,
        in_specs=[smem] * 3 + [vmem] * (2 + len(low)),
        out_specs=[vmem] * 4,
        out_shape=[
            jax.ShapeDtypeStruct((tokens, HDIM), BF),
            jax.ShapeDtypeStruct((tokens, HDIM), BF),
            jax.ShapeDtypeStruct((3, tokens, HDIM), BF),
            jax.ShapeDtypeStruct((8, tokens), F32),
        ],
        scratch_shapes=[pltpu.VMEM((2, 3, tokens, HDIM), BF)],
        cost_estimate=pl.CostEstimate(
            flops=12 * tokens * tokens * HDIM,
            transcendentals=3 * tokens * tokens,
            bytes_accessed=8 * MIB,
        ),
        compiler_params=pltpu.CompilerParams(vmem_limit_bytes=56 * MIB),
        name="attention_forward",
    )(place, scale, inverse, heads, up, *low)


def backward_kernel(
    n_fast, place_ref, student_ref, upstream_ref, stats_ref, up_ref, *refs
):
    low_refs, back_refs = refs[:n_fast], refs[n_fast : 2 * n_fast]
    grad_up_ref, dq_ref, dk_ref, dv_ref = refs[2 * n_fast :]
    tokens = student_ref.shape[1]
    n_slow, rows, _ = low_refs[0].shape
    here_slow, here_fast = place_ref[0], place_ref[1]
    step_rows = 256
    dk_ref[...] = jnp.zeros_like(dk_ref)
    dv_ref[...] = jnp.zeros_like(dv_ref)

    def one_block(step, carry):
        here = pl.ds(pl.multiple_of(step * step_rows, step_rows), step_rows)
        query = student_ref[0, here]
        upstream = upstream_ref[here]
        key = student_ref[1]
        level = stats_ref[0:1, here]
        center = stats_ref[1:2, here]
        prob = jnp.exp2(dot(key, query, NT) * SCALE2 - level)
        dv_ref[...] += dot(prob.astype(BF), upstream)
        dprob = dot(student_ref[2], upstream, NT)
        dscore = (prob * (dprob - center)).astype(BF)
        dk_ref[...] += dot(dscore, query)
        dq_ref[here] = dot(dscore, key, TN)
        return carry

    lax.fori_loop(0, tokens // step_rows, one_block, 0)
    for part, (ref, factor) in enumerate(((dq_ref, FACTOR), (dk_ref, FACTOR), (dv_ref, 1.0))):
        up = up_ref[part]
        total = jnp.zeros((RANK, HDIM), F32)
        columns = slice(part * RANK, (part + 1) * RANK)
        for fast in range(n_fast):
            for slow in range(n_slow):
                ahead = lax.rem(here_slow + slow, n_slow) * n_fast + lax.rem(
                    here_fast + fast, n_fast
                )
                behind = lax.rem(here_slow - slow + n_slow, n_slow) * n_fast + lax.rem(
                    here_fast - fast + n_fast, n_fast
                )
                grad = ref[pl.ds(pl.multiple_of(ahead * rows, rows), rows)] * factor
                back_refs[fast][slow, :, columns] = dot(grad.astype(BF), up, NT).astype(BF)
                grad = ref[pl.ds(pl.multiple_of(behind * rows, rows), rows)] * factor
                total += dot(low_refs[fast][slow, :, columns], grad.astype(BF), TN)
        grad_up_ref[part] = total.astype(BF)


def backward(place, student, upstream, stats, up, low):
    tokens, n_fast = student.shape[1], len(low)
    vmem = pl.BlockSpec(memory_space=pltpu.VMEM)
    return pl.pallas_call(
        functools.partial(backward_kernel, n_fast),
        in_specs=[pl.BlockSpec(memory_space=pltpu.SMEM)] + [vmem] * (4 + n_fast),
        out_specs=[vmem] * (n_fast + 1),
        out_shape=[jax.ShapeDtypeStruct(low[0].shape, BF)] * n_fast
        + [
            jax.ShapeDtypeStruct((3, RANK, HDIM), BF),
        ],
        scratch_shapes=[pltpu.VMEM((tokens, HDIM), F32)] * 3,
        cost_estimate=pl.CostEstimate(
            flops=10 * tokens * tokens * HDIM,
            transcendentals=tokens * tokens,
            bytes_accessed=6 * MIB,
        ),
        compiler_params=pltpu.CompilerParams(vmem_limit_bytes=56 * MIB),
        name="attention_backward",
    )(place, student, upstream, stats, up, *low)


def body(
    teacher_query,
    teacher_key,
    teacher_value,
    hidden,
    adapter_down_weight,
    adapter_up_weight,
    guidance_index,
    timestep_index,
):
    n_cfg, n_slow, n_fast = (lax.axis_size(a) for a in ("cfg", "z", "y"))
    n_x, n_core = (lax.axis_size(a) for a in ("x", "core"))
    cfg_index = lax.axis_index("cfg")
    seq_index = lax.axis_index(("z", "y"))
    features = hidden[0, 0]
    rows, width = features.shape
    tokens = rows * n_slow * n_fast
    total_rows = n_cfg * n_x * n_core * tokens

    packed = packed_by_head(teacher_query[0, :, 0], teacher_key[0, :, 0], teacher_value[0, :, 0])
    heads = exchange(packed, ("cfg", "z", "y"))
    heads = heads.reshape(n_cfg, n_slow * n_fast, 3, rows, HDIM)

    scale = 1.0 + 0.5 * lax.dynamic_slice(guidance_index[:, 0], (cfg_index,), (1,)).astype(F32)
    time = (lax.dynamic_slice(timestep_index[:, 0], (cfg_index,), (1,)).astype(F32) + 0.5) / TSTEPS
    rank_index = jnp.arange(1, RANK + 1).astype(F32)
    modulation = 1.0 + 0.5 * jnp.cos(math.pi * rank_index * time + 0.25 * rank_index * scale)

    low = jnp.einsum("cl,elj->cej", features, adapter_down_weight, preferred_element_type=F32)
    low = (low * modulation).astype(BF).reshape(rows, 3 * RANK)
    low_all = from_each(jnp.stack(from_each(low, "z")), "y")

    groups = n_cfg * n_slow
    part_cols = width // (groups * n_fast)
    spread = parts_ahead(features.reshape(rows, groups, n_fast, part_cols), "y", 2)
    spread = [part.reshape(rows, groups * part_cols) for part in spread]
    columns = jnp.concatenate(
        [spread[0]] + [shifted(spread[d], "y", d) for d in range(1, n_fast)]
    )

    place = jnp.stack([lax.axis_index("z"), lax.axis_index("y")]).astype(jnp.int32)
    up = lax.dynamic_slice_in_dim(adapter_up_weight, seq_index * HDIM, HDIM, 2)
    inverse = jnp.full((1,), 1.0 / math.sqrt(total_rows), F32)
    out, upstream, student, stats = forward(place, scale, inverse, heads, up, low_all)
    tokens_out = exchange(out.reshape(n_slow * n_fast, rows, HDIM), ("z", "y"))
    student_out = jnp.moveaxis(tokens_out, 0, 1).reshape(rows, -1)

    *back, up_partial = backward(place, student, upstream, stats, up, low_all)
    back = summed_parts(back, "y").astype(BF)
    back = summed_parts([back[d] for d in range(n_slow)], "z")
    low_grad = (back.reshape(rows, 3, RANK) * modulation).astype(BF).reshape(rows, 3 * RANK)
    low_grads = jnp.concatenate(from_each(low_grad, "y"))
    down = dot(columns, low_grads, TN).astype(BF)
    down = down.reshape(n_cfg, n_slow, n_x, n_core, -1, 3 * RANK).transpose(3, 2, 0, 1, 4, 5)
    down = reduced(down, ("core", "x", "cfg", "z"))
    grad_down = jnp.moveaxis(down.reshape(-1, 3, RANK), 1, 0)

    up_blocks = up_partial.reshape(3, n_cfg, n_x, n_core, -1, HDIM).transpose(3, 2, 1, 0, 4, 5)
    grad_up = reduced(up_blocks, ("core", "x", "cfg"))
    return student_out[None, None], grad_down, grad_up


def solution(mesh):
    sizes = {"cfg": 2, "z": 4, "y": 4, "x": 4, "core": 2}
    mesh = Mesh(mesh.devices.reshape(tuple(sizes.values())), tuple(sizes))
    seq, dp = ("z", "y"), ("x", "core")
    teacher = P("cfg", None, dp, seq, None)
    return jax.shard_map(
        body,
        mesh=mesh,
        in_specs=(
            teacher,
            teacher,
            teacher,
            P("cfg", dp, seq, None),
            P(),
            P(),
            P(None, dp),
            P(None, dp),
        ),
        out_specs=(
            P("cfg", dp, seq, None),
            P(None, ("cfg", *seq, *dp), None),
            P(None, ("cfg", *dp), seq),
        ),
        check_vma=False,
    )
```

```python
import functools
import math

import jax
import jax.numpy as jnp
from jax import lax
from jax.experimental import pallas as pl
from jax.experimental.pallas import tpu as pltpu
from jax.sharding import Mesh
from jax.sharding import PartitionSpec as P

HDIM = 128
RANK = 128
TSTEPS = 1000
FACTOR = HDIM ** (-0.5)
LOG2E = math.log2(math.e)
SCALE2 = FACTOR * LOG2E
BF = jnp.bfloat16
F32 = jnp.float32
NT = (((1,), (1,)), ((), ()))
TN = (((0,), (0,)), ((), ()))
MIB = 1 << 20


def dot(a, b, dims=(((1,), (0,)), ((), ()))):
    return lax.dot_general(a, b, dims, preferred_element_type=F32)


def exchange(value, axes):
    return lax.all_to_all(value, axes, split_axis=0, concat_axis=0, tiled=True)


def shifted(value, axis, distance):
    size = lax.axis_size(axis)
    return lax.ppermute(value, axis, [(i, (i + distance) % size) for i in range(size)])


def from_each(value, axis):
    return [value] + [shifted(value, axis, d) for d in range(1, lax.axis_size(axis))]


def summed_parts(parts, axis):
    total = parts[0].astype(F32)
    for d in range(1, lax.axis_size(axis)):
        total = total + shifted(parts[d].astype(BF), axis, d).astype(F32)
    return total


def parts_ahead(value, axis, dim):
    size, here = lax.axis_size(axis), lax.axis_index(axis)
    return [
        lax.dynamic_index_in_dim(value, (here + d) % size, dim, keepdims=False)
        for d in range(size)
    ]


def summed_over_pair(value, slow, fast):
    n_slow, n_fast = lax.axis_size(slow), lax.axis_size(fast)
    total = None
    for ds, across in enumerate(parts_ahead(value, slow, 0)):
        for df, part in enumerate(parts_ahead(across, fast, 0)):
            if ds or df:
                pairs = [
                    (i * n_fast + j, (i + ds) % n_slow * n_fast + (j + df) % n_fast)
                    for i in range(n_slow)
                    for j in range(n_fast)
                ]
                part = lax.ppermute(part.astype(BF), (slow, fast), pairs)
            total = part.astype(F32) if total is None else total + part.astype(F32)
    return total


def pack_kernel(q_ref, k_ref, v_ref, out_ref):
    heads = out_ref.shape[0]
    for part, ref in enumerate((q_ref, k_ref, v_ref)):
        for head in range(heads):
            out_ref[head, part] = ref[0, :, head * HDIM : (head + 1) * HDIM]


def packed_by_head(q, k, v):
    halves, rows, columns = q.shape
    heads = columns // HDIM
    spec = pl.BlockSpec((1, rows, columns), lambda i: (i, 0, 0))
    return pl.pallas_call(
        pack_kernel,
        grid=(halves,),
        in_specs=[spec] * 3,
        out_specs=pl.BlockSpec((heads, 3, rows, HDIM), lambda i: (i, 0, 0, 0)),
        out_shape=jax.ShapeDtypeStruct((halves * heads, 3, rows, HDIM), q.dtype),
        cost_estimate=pl.CostEstimate(flops=0, transcendentals=0, bytes_accessed=12 * q.size),
        name="pack_heads",
    )(q, k, v)


def softmax_rows(query, key):
    scores = dot(query, key, NT)
    highest = jnp.max(scores, axis=-1, keepdims=True)
    raised = jnp.exp2((scores - highest) * SCALE2)
    total = jnp.sum(raised, axis=-1, keepdims=True)
    return raised.astype(BF), highest, total


def teacher_kernel(scale_ref, heads_ref, target_ref, keys_ref):
    blocks, rows = heads_ref.shape[1], heads_ref.shape[3]
    tokens = blocks * rows
    scale = scale_ref[0]
    for one in range(2):
        for part in range(3):
            for block in range(blocks):
                keys_ref[one, part, block * rows : (block + 1) * rows] = heads_ref[one, block, part]
    step_rows = 256

    def one_block(step, carry):
        here = pl.ds(pl.multiple_of(step * step_rows, step_rows), step_rows)
        outs = []
        for one in range(2):
            raised, _, total = softmax_rows(keys_ref[one, 0, here], keys_ref[one, 1])
            attended = dot(raised, keys_ref[one, 2]) / total
            outs.append(attended.astype(BF).astype(F32))
        target_ref[here] = outs[1] + scale * (outs[0] - outs[1])
        return carry

    lax.fori_loop(0, tokens // step_rows, one_block, 0)


def teacher(scale, heads):
    tokens = heads.shape[1] * heads.shape[3]
    vmem = pl.BlockSpec(memory_space=pltpu.VMEM)
    return pl.pallas_call(
        teacher_kernel,
        in_specs=[pl.BlockSpec(memory_space=pltpu.SMEM), vmem],
        out_specs=vmem,
        out_shape=jax.ShapeDtypeStruct((tokens, HDIM), F32),
        scratch_shapes=[pltpu.VMEM((2, 3, tokens, HDIM), BF)],
        cost_estimate=pl.CostEstimate(
            flops=8 * tokens * tokens * HDIM,
            transcendentals=2 * tokens * tokens,
            bytes_accessed=4 * MIB,
        ),
        compiler_params=pltpu.CompilerParams(vmem_limit_bytes=48 * MIB),
        name="teacher_forward",
    )(scale, heads)


def student_kernel(n_fast, place_ref, inv_ref, heads_ref, target_ref, up_ref, *refs):
    low_refs = refs[:n_fast]
    out_ref, upstream_ref, student_ref, stats_ref = refs[n_fast:]
    rows = heads_ref.shape[3]
    tokens = out_ref.shape[0]
    n_slow = low_refs[0].shape[0]
    here_slow, here_fast = place_ref[0], place_ref[1]
    inverse = inv_ref[0]

    for part in range(3):
        up = up_ref[part]
        for fast in range(n_fast):
            for slow in range(n_slow):
                block = lax.rem(here_slow - slow + n_slow, n_slow) * n_fast + lax.rem(
                    here_fast - fast + n_fast, n_fast
                )
                columns = slice(part * RANK, (part + 1) * RANK)
                adapted = dot(low_refs[fast][slow, :, columns], up)
                frozen = heads_ref[0, block, part].astype(F32)
                where = pl.ds(pl.multiple_of(block * rows, rows), rows)
                student_ref[part, where] = (frozen + adapted).astype(BF)
    step_rows = 256

    def one_block(step, carry):
        here = pl.ds(pl.multiple_of(step * step_rows, step_rows), step_rows)
        raised, highest, total = softmax_rows(student_ref[0, here], student_ref[1])
        attended = dot(raised, student_ref[2]) / total
        rounded = attended.astype(BF)
        out_ref[here] = rounded
        upstream = ((rounded.astype(F32) - target_ref[here]) * inverse).astype(BF)
        upstream_ref[here] = upstream
        level = highest * SCALE2 + jnp.log2(total)
        center = jnp.sum(attended * upstream.astype(F32), axis=-1, keepdims=True)
        stats_ref[0:1, here] = jnp.transpose(jnp.broadcast_to(level, (step_rows, HDIM)))[0:1]
        stats_ref[1:2, here] = jnp.transpose(jnp.broadcast_to(center, (step_rows, HDIM)))[0:1]
        return carry

    stats_ref[...] = jnp.zeros_like(stats_ref)
    lax.fori_loop(0, tokens // step_rows, one_block, 0)


def student_forward(place, inverse, heads, target, up, low):
    tokens = target.shape[0]
    one_pass = (1, *heads.shape[1:])
    vmem = pl.BlockSpec(memory_space=pltpu.VMEM)
    smem = pl.BlockSpec(memory_space=pltpu.SMEM)
    return pl.pallas_call(
        functools.partial(student_kernel, len(low)),
        grid=(1,),
        in_specs=[smem, smem, pl.BlockSpec(one_pass, lambda i: (0, 0, 0, 0, 0))]
        + [vmem] * (2 + len(low)),
        out_specs=[vmem] * 4,
        out_shape=[
            jax.ShapeDtypeStruct((tokens, HDIM), BF),
            jax.ShapeDtypeStruct((tokens, HDIM), BF),
            jax.ShapeDtypeStruct((3, tokens, HDIM), BF),
            jax.ShapeDtypeStruct((8, tokens), F32),
        ],
        cost_estimate=pl.CostEstimate(
            flops=4 * tokens * tokens * HDIM,
            transcendentals=tokens * tokens,
            bytes_accessed=6 * MIB,
        ),
        compiler_params=pltpu.CompilerParams(vmem_limit_bytes=48 * MIB),
        name="student_forward",
    )(place, inverse, heads, target, up, *low)


def backward_kernel(
    n_fast, place_ref, student_ref, upstream_ref, stats_ref, up_ref, *refs
):
    low_refs, back_refs = refs[:n_fast], refs[n_fast : 2 * n_fast]
    grad_up_ref, dq_ref, dk_ref, dv_ref = refs[2 * n_fast :]
    tokens = student_ref.shape[1]
    n_slow, rows, _ = low_refs[0].shape
    here_slow, here_fast = place_ref[0], place_ref[1]
    step_rows = 256
    dk_ref[...] = jnp.zeros_like(dk_ref)
    dv_ref[...] = jnp.zeros_like(dv_ref)

    def one_block(step, carry):
        here = pl.ds(pl.multiple_of(step * step_rows, step_rows), step_rows)
        query = student_ref[0, here]
        upstream = upstream_ref[here]
        key = student_ref[1]
        level = stats_ref[0:1, here]
        center = stats_ref[1:2, here]
        prob = jnp.exp2(dot(key, query, NT) * SCALE2 - level)
        dv_ref[...] += dot(prob.astype(BF), upstream)
        dprob = dot(student_ref[2], upstream, NT)
        dscore = (prob * (dprob - center)).astype(BF)
        dk_ref[...] += dot(dscore, query)
        dq_ref[here] = dot(dscore, key, TN)
        return carry

    lax.fori_loop(0, tokens // step_rows, one_block, 0)
    for part, (ref, factor) in enumerate(((dq_ref, FACTOR), (dk_ref, FACTOR), (dv_ref, 1.0))):
        up = up_ref[part]
        total = jnp.zeros((RANK, HDIM), F32)
        columns = slice(part * RANK, (part + 1) * RANK)
        for fast in range(n_fast):
            for slow in range(n_slow):
                ahead = lax.rem(here_slow + slow, n_slow) * n_fast + lax.rem(
                    here_fast + fast, n_fast
                )
                behind = lax.rem(here_slow - slow + n_slow, n_slow) * n_fast + lax.rem(
                    here_fast - fast + n_fast, n_fast
                )
                grad = ref[pl.ds(pl.multiple_of(ahead * rows, rows), rows)] * factor
                back_refs[fast][slow, :, columns] = dot(grad.astype(BF), up, NT).astype(BF)
                grad = ref[pl.ds(pl.multiple_of(behind * rows, rows), rows)] * factor
                total += dot(low_refs[fast][slow, :, columns], grad.astype(BF), TN)
        grad_up_ref[part] = total.astype(BF)


def backward(place, student, upstream, stats, up, low):
    tokens, n_fast = student.shape[1], len(low)
    vmem = pl.BlockSpec(memory_space=pltpu.VMEM)
    return pl.pallas_call(
        functools.partial(backward_kernel, n_fast),
        in_specs=[pl.BlockSpec(memory_space=pltpu.SMEM)] + [vmem] * (4 + n_fast),
        out_specs=[vmem] * (n_fast + 1),
        out_shape=[jax.ShapeDtypeStruct(low[0].shape, BF)] * n_fast
        + [
            jax.ShapeDtypeStruct((3, RANK, HDIM), BF),
        ],
        scratch_shapes=[pltpu.VMEM((tokens, HDIM), F32)] * 3,
        cost_estimate=pl.CostEstimate(
            flops=10 * tokens * tokens * HDIM,
            transcendentals=tokens * tokens,
            bytes_accessed=6 * MIB,
        ),
        compiler_params=pltpu.CompilerParams(vmem_limit_bytes=56 * MIB),
        name="attention_backward",
    )(place, student, upstream, stats, up, *low)


def body(
    teacher_query,
    teacher_key,
    teacher_value,
    hidden,
    adapter_down_weight,
    adapter_up_weight,
    guidance_index,
    timestep_index,
):
    n_cfg, n_slow, n_fast = (lax.axis_size(a) for a in ("cfg", "z", "y"))
    n_x, n_core = (lax.axis_size(a) for a in ("x", "core"))
    cfg_index = lax.axis_index("cfg")
    seq_index = lax.axis_index(("z", "y"))
    features = hidden[0, 0]
    rows, width = features.shape
    tokens = rows * n_slow * n_fast
    total_rows = n_cfg * n_x * n_core * tokens

    packed = packed_by_head(teacher_query[0, :, 0], teacher_key[0, :, 0], teacher_value[0, :, 0])
    heads = exchange(packed, ("cfg", "z", "y"))
    heads = heads.reshape(n_cfg, n_slow * n_fast, 3, rows, HDIM)

    scale = 1.0 + 0.5 * lax.dynamic_slice(guidance_index[:, 0], (cfg_index,), (1,)).astype(F32)
    time = (lax.dynamic_slice(timestep_index[:, 0], (cfg_index,), (1,)).astype(F32) + 0.5) / TSTEPS
    rank_index = jnp.arange(1, RANK + 1).astype(F32)
    modulation = 1.0 + 0.5 * jnp.cos(math.pi * rank_index * time + 0.25 * rank_index * scale)

    low = jnp.einsum("cl,elj->cej", features, adapter_down_weight, preferred_element_type=F32)
    low = (low * modulation).astype(BF).reshape(rows, 3 * RANK)
    low_slow = jnp.stack(from_each(low, "z"))

    groups = n_cfg * n_slow
    part_cols = width // (groups * n_fast)
    spread = parts_ahead(features.reshape(rows, groups, n_fast, part_cols), "y", 2)
    spread = [part.reshape(rows, groups * part_cols) for part in spread]
    columns = [spread[0]] + [shifted(spread[d], "y", d) for d in range(1, n_fast)]

    place = jnp.stack([lax.axis_index("z"), lax.axis_index("y")]).astype(jnp.int32)
    up = lax.dynamic_slice_in_dim(adapter_up_weight, seq_index * HDIM, HDIM, 2)
    inverse = jnp.full((1,), 1.0 / math.sqrt(total_rows), F32)

    heads, low_slow, up, place, *columns = lax.optimization_barrier(
        (heads, low_slow, up, place, *columns)
    )
    low_all = from_each(low_slow, "y")
    target = teacher(scale, heads)
    target, *low_all = lax.optimization_barrier((target, *low_all))
    out, upstream, student, stats = student_forward(place, inverse, heads, target, up, low_all)
    tokens_out = exchange(out.reshape(n_slow * n_fast, rows, HDIM), ("z", "y"))

    *back, up_partial = backward(place, student, upstream, stats, up, low_all)
    tokens_out, up_partial, *back = lax.optimization_barrier((tokens_out, up_partial, *back))
    student_out = jnp.moveaxis(tokens_out, 0, 1).reshape(rows, -1)

    owners = n_cfg * n_x * n_core
    up_blocks = jnp.moveaxis(up_partial.reshape(3, owners, RANK // owners, HDIM), 1, 0)
    grad_up = exchange(up_blocks, ("cfg", "x", "core"))

    back = summed_parts(back, "y").astype(BF)
    back = summed_parts([back[d] for d in range(n_slow)], "z")
    low_grad = (back.reshape(rows, 3, RANK) * modulation).astype(BF).reshape(rows, 3 * RANK)
    low_grad, grad_up = lax.optimization_barrier((low_grad, grad_up))
    grad_up = grad_up.astype(F32).sum(axis=0)
    low_grads = jnp.concatenate(from_each(low_grad, "y"))
    down = dot(jnp.concatenate(columns), low_grads, TN).astype(BF)
    down = down.reshape(n_cfg, n_slow, n_x, n_core, -1, 3 * RANK).transpose(2, 3, 0, 1, 4, 5)
    down = summed_over_pair(down, "x", "core")
    down = summed_over_pair(down, "cfg", "z")
    grad_down = jnp.moveaxis(down.reshape(-1, 3, RANK), 1, 0)
    return student_out[None, None], grad_down, grad_up


def solution(mesh):
    sizes = {"cfg": 2, "z": 4, "y": 4, "x": 4, "core": 2}
    mesh = Mesh(mesh.devices.reshape(tuple(sizes.values())), tuple(sizes))
    seq, dp = ("z", "y"), ("x", "core")
    teacher = P("cfg", None, dp, seq, None)
    return jax.shard_map(
        body,
        mesh=mesh,
        in_specs=(
            teacher,
            teacher,
            teacher,
            P("cfg", dp, seq, None),
            P(),
            P(),
            P(None, dp),
            P(None, dp),
        ),
        out_specs=(
            P("cfg", dp, seq, None),
            P(None, ("cfg", *seq, *dp), None),
            P(None, ("cfg", *dp), seq),
        ),
        check_vma=False,
    )
```

```python
import functools
import math

import jax
import jax.numpy as jnp
from jax import lax
from jax.experimental import pallas as pl
from jax.experimental.pallas import tpu as pltpu
from jax.sharding import Mesh
from jax.sharding import PartitionSpec as P

HDIM = 128
RANK = 128
TSTEPS = 1000
FACTOR = HDIM ** (-0.5)
LOG2E = math.log2(math.e)
SCALE2 = FACTOR * LOG2E
BF = jnp.bfloat16
F32 = jnp.float32
NT = (((1,), (1,)), ((), ()))
TN = (((0,), (0,)), ((), ()))
MIB = 1 << 20


def dot(a, b, dims=(((1,), (0,)), ((), ()))):
    return lax.dot_general(a, b, dims, preferred_element_type=F32)


def exchange(value, axes):
    return lax.all_to_all(value, axes, split_axis=0, concat_axis=0, tiled=True)


def shifted(value, axis, distance):
    size = lax.axis_size(axis)
    return lax.ppermute(value, axis, [(i, (i + distance) % size) for i in range(size)])


def from_each(value, axis):
    return [value] + [shifted(value, axis, d) for d in range(1, lax.axis_size(axis))]


def summed_parts(parts, axis):
    total = parts[0].astype(F32)
    for d in range(1, lax.axis_size(axis)):
        total = total + shifted(parts[d].astype(BF), axis, d).astype(F32)
    return total


def parts_ahead(value, axis, dim):
    size, here = lax.axis_size(axis), lax.axis_index(axis)
    return [
        lax.dynamic_index_in_dim(value, (here + d) % size, dim, keepdims=False)
        for d in range(size)
    ]


def reduced(value, axes):
    for axis in axes:
        value = summed_parts(parts_ahead(value, axis, 0), axis)
    return value


def pack_kernel(q_ref, k_ref, v_ref, out_ref):
    heads = out_ref.shape[0]
    for part, ref in enumerate((q_ref, k_ref, v_ref)):
        for head in range(heads):
            out_ref[head, part] = ref[0, :, head * HDIM : (head + 1) * HDIM]


def packed_by_head(q, k, v):
    halves, rows, columns = q.shape
    heads = columns // HDIM
    spec = pl.BlockSpec((1, rows, columns), lambda i: (i, 0, 0))
    return pl.pallas_call(
        pack_kernel,
        grid=(halves,),
        in_specs=[spec] * 3,
        out_specs=pl.BlockSpec((heads, 3, rows, HDIM), lambda i: (i, 0, 0, 0)),
        out_shape=jax.ShapeDtypeStruct((halves * heads, 3, rows, HDIM), q.dtype),
        cost_estimate=pl.CostEstimate(flops=0, transcendentals=0, bytes_accessed=12 * q.size),
        name="pack_heads",
    )(q, k, v)


def with_ones(ref, values):
    ref[:, :HDIM] = values
    ref[:, HDIM:] = jnp.ones_like(values)


def attended_rows(scores, value_ref):
    highest = jnp.max(scores, axis=-1, keepdims=True)
    raised = jnp.exp2((scores - highest) * SCALE2).astype(BF)
    both = dot(raised, value_ref[...])
    total = both[:, HDIM:]
    return both[:, :HDIM] / total, highest, total


def teacher_kernel(scale_ref, heads_ref, target_ref, query_ref, key_ref, value_ref, scores_ref):
    blocks, rows = heads_ref.shape[1], heads_ref.shape[3]
    tokens = blocks * rows
    scale = scale_ref[0]
    for one in range(2):
        for block in range(blocks):
            where = slice(block * rows, (block + 1) * rows)
            query_ref[one, where] = heads_ref[one, block, 0]
            key_ref[one, :, where] = jnp.transpose(heads_ref[one, block, 1])
            with_ones(value_ref.at[one, where], heads_ref[one, block, 2])
    step_rows = scores_ref.shape[1]
    steps = tokens // step_rows

    def rows_of(step):
        return pl.ds(pl.multiple_of(step * step_rows, step_rows), step_rows)

    def put_scores(step, one):
        scores_ref[one] = dot(query_ref[one, rows_of(step)], key_ref[one])

    def rounded(one):
        return attended_rows(scores_ref[one], value_ref.at[one])[0].astype(BF).astype(F32)

    def one_block(step, carry):
        put_scores(step, 1)
        conditional = rounded(0)
        put_scores(jnp.minimum(step + 1, steps - 1), 0)
        unconditional = rounded(1)
        target_ref[rows_of(step)] = unconditional + scale * (conditional - unconditional)
        return carry

    put_scores(0, 0)
    lax.fori_loop(0, steps, one_block, 0)


def teacher(scale, heads):
    tokens = heads.shape[1] * heads.shape[3]
    vmem = pl.BlockSpec(memory_space=pltpu.VMEM)
    return pl.pallas_call(
        teacher_kernel,
        in_specs=[pl.BlockSpec(memory_space=pltpu.SMEM), vmem],
        out_specs=vmem,
        out_shape=jax.ShapeDtypeStruct((tokens, HDIM), F32),
        scratch_shapes=[
            pltpu.VMEM((2, tokens, HDIM), BF),
            pltpu.VMEM((2, HDIM, tokens), BF),
            pltpu.VMEM((2, tokens, 2 * HDIM), BF),
            pltpu.VMEM((2, 256, tokens), F32),
        ],
        cost_estimate=pl.CostEstimate(
            flops=8 * tokens * tokens * HDIM,
            transcendentals=2 * tokens * tokens,
            bytes_accessed=4 * MIB,
        ),
        compiler_params=pltpu.CompilerParams(vmem_limit_bytes=24 * MIB),
        name="teacher_forward",
    )(scale, heads)


def student_kernel(n_fast, place_ref, inv_ref, heads_ref, target_ref, up_ref, *refs):
    low_refs = refs[:n_fast]
    out_ref, upstream_ref, student_ref, stats_ref, key_ref, value_ref, scores_ref = refs[n_fast:]
    rows = heads_ref.shape[3]
    tokens = out_ref.shape[0]
    n_slow = low_refs[0].shape[0]
    here_slow, here_fast = place_ref[0], place_ref[1]
    inverse = inv_ref[0]

    for part in range(3):
        up = up_ref[part]
        for fast in range(n_fast):
            low = low_refs[fast][:, :, part * RANK : (part + 1) * RANK]
            adapted = dot(low.reshape(n_slow * rows, RANK), up)
            for slow in range(n_slow):
                block = lax.rem(here_slow - slow + n_slow, n_slow) * n_fast + lax.rem(
                    here_fast - fast + n_fast, n_fast
                )
                frozen = heads_ref[0, block, part].astype(F32)
                where = pl.ds(pl.multiple_of(block * rows, rows), rows)
                student_ref[part, where] = (
                    frozen + adapted[slow * rows : (slow + 1) * rows]
                ).astype(BF)
    for block in range(n_slow * n_fast):
        where = slice(block * rows, (block + 1) * rows)
        key_ref[:, where] = jnp.transpose(student_ref[1, where])
        with_ones(value_ref.at[where], student_ref[2, where])
    step_rows = scores_ref.shape[1]
    steps = tokens // step_rows

    def rows_of(step):
        return pl.ds(pl.multiple_of(step * step_rows, step_rows), step_rows)

    def put_scores(step, slot):
        scores_ref[slot] = dot(student_ref[0, rows_of(step)], key_ref[...])

    def finish(step, slot):
        here = rows_of(step)
        attended, highest, total = attended_rows(scores_ref[slot], value_ref)
        rounded = attended.astype(BF)
        out_ref[here] = rounded
        upstream = ((rounded.astype(F32) - target_ref[here]) * inverse).astype(BF)
        upstream_ref[here] = upstream
        level = highest * SCALE2 + jnp.log2(total)
        center = jnp.sum(attended * upstream.astype(F32), axis=-1, keepdims=True)
        stats_ref[0:1, here] = jnp.transpose(level)[0:1]
        stats_ref[1:2, here] = jnp.transpose(jnp.broadcast_to(center, (step_rows, HDIM)))[0:1]

    def two_blocks(pair, carry):
        put_scores(2 * pair + 1, 1)
        finish(2 * pair, 0)
        put_scores(jnp.minimum(2 * pair + 2, steps - 1), 0)
        finish(2 * pair + 1, 1)
        return carry

    stats_ref[...] = jnp.zeros_like(stats_ref)
    put_scores(0, 0)
    lax.fori_loop(0, steps // 2, two_blocks, 0)


def student_forward(place, inverse, heads, target, up, low):
    tokens = target.shape[0]
    one_pass = (1, *heads.shape[1:])
    vmem = pl.BlockSpec(memory_space=pltpu.VMEM)
    smem = pl.BlockSpec(memory_space=pltpu.SMEM)
    return pl.pallas_call(
        functools.partial(student_kernel, len(low)),
        grid=(1,),
        in_specs=[smem, smem, pl.BlockSpec(one_pass, lambda i: (0, 0, 0, 0, 0))]
        + [vmem] * (2 + len(low)),
        out_specs=[vmem] * 4,
        out_shape=[
            jax.ShapeDtypeStruct((tokens, HDIM), BF),
            jax.ShapeDtypeStruct((tokens, HDIM), BF),
            jax.ShapeDtypeStruct((3, tokens, HDIM), BF),
            jax.ShapeDtypeStruct((8, tokens), F32),
        ],
        scratch_shapes=[
            pltpu.VMEM((HDIM, tokens), BF),
            pltpu.VMEM((tokens, 2 * HDIM), BF),
            pltpu.VMEM((2, 256, tokens), F32),
        ],
        cost_estimate=pl.CostEstimate(
            flops=4 * tokens * tokens * HDIM,
            transcendentals=tokens * tokens,
            bytes_accessed=6 * MIB,
        ),
        compiler_params=pltpu.CompilerParams(vmem_limit_bytes=24 * MIB),
        name="student_forward",
    )(place, inverse, heads, target, up, *low)


def backward_kernel(
    n_fast, place_ref, student_ref, upstream_ref, stats_ref, up_ref, *refs
):
    low_refs, back_refs = refs[:n_fast], refs[n_fast : 2 * n_fast]
    grad_up_ref, dq_ref, dk_ref, dv_ref, flat_ref = refs[2 * n_fast :]
    tokens = student_ref.shape[1]
    n_slow, rows, _ = low_refs[0].shape
    here_slow, here_fast = place_ref[0], place_ref[1]
    step_rows = 512
    dk_ref[...] = jnp.zeros_like(dk_ref)
    dv_ref[...] = jnp.zeros_like(dv_ref)
    flat_ref[...] = jnp.transpose(student_ref[1])

    def one_block(step, carry):
        here = pl.ds(pl.multiple_of(step * step_rows, step_rows), step_rows)
        query = student_ref[0, here]
        upstream = upstream_ref[here]
        level = stats_ref[0:1, here]
        center = stats_ref[1:2, here]
        prob = jnp.exp2(dot(student_ref[1], query, NT) * SCALE2 - level)
        dv_ref[...] += dot(prob.astype(BF), upstream)
        dprob = dot(student_ref[2], upstream, NT)
        dscore = (prob * (dprob - center)).astype(BF)
        dk_ref[...] += dot(dscore, query)
        dq_ref[here] = jnp.transpose(dot(flat_ref[...], dscore))
        return carry

    lax.fori_loop(0, tokens // step_rows, one_block, 0)
    for part, (ref, factor) in enumerate(((dq_ref, FACTOR), (dk_ref, FACTOR), (dv_ref, 1.0))):
        up = up_ref[part]
        total = jnp.zeros((RANK, HDIM), F32)
        columns = slice(part * RANK, (part + 1) * RANK)
        for fast in range(n_fast):
            for slow in range(n_slow):
                ahead = lax.rem(here_slow + slow, n_slow) * n_fast + lax.rem(
                    here_fast + fast, n_fast
                )
                behind = lax.rem(here_slow - slow + n_slow, n_slow) * n_fast + lax.rem(
                    here_fast - fast + n_fast, n_fast
                )
                grad = ref[pl.ds(pl.multiple_of(ahead * rows, rows), rows)] * factor
                back_refs[fast][slow, :, columns] = dot(grad.astype(BF), up, NT).astype(BF)
                grad = ref[pl.ds(pl.multiple_of(behind * rows, rows), rows)] * factor
                total += dot(low_refs[fast][slow, :, columns], grad.astype(BF), TN)
        grad_up_ref[:, part * HDIM : (part + 1) * HDIM] = total.astype(BF)


def backward(place, student, upstream, stats, up, low):
    tokens, n_fast = student.shape[1], len(low)
    vmem = pl.BlockSpec(memory_space=pltpu.VMEM)
    return pl.pallas_call(
        functools.partial(backward_kernel, n_fast),
        in_specs=[pl.BlockSpec(memory_space=pltpu.SMEM)] + [vmem] * (4 + n_fast),
        out_specs=[vmem] * (n_fast + 1),
        out_shape=[jax.ShapeDtypeStruct(low[0].shape, BF)] * n_fast
        + [
            jax.ShapeDtypeStruct((RANK, 3 * HDIM), BF),
        ],
        scratch_shapes=[pltpu.VMEM((tokens, HDIM), F32)] * 3 + [pltpu.VMEM((HDIM, tokens), BF)],
        cost_estimate=pl.CostEstimate(
            flops=10 * tokens * tokens * HDIM,
            transcendentals=tokens * tokens,
            bytes_accessed=6 * MIB,
        ),
        compiler_params=pltpu.CompilerParams(vmem_limit_bytes=40 * MIB),
        name="attention_backward",
    )(place, student, upstream, stats, up, *low)


def body(
    teacher_query,
    teacher_key,
    teacher_value,
    hidden,
    adapter_down_weight,
    adapter_up_weight,
    guidance_index,
    timestep_index,
):
    n_cfg, n_slow, n_fast = (lax.axis_size(a) for a in ("cfg", "z", "y"))
    n_x, n_core = (lax.axis_size(a) for a in ("x", "core"))
    cfg_index = lax.axis_index("cfg")
    seq_index = lax.axis_index(("z", "y"))
    features = hidden[0, 0]
    rows, width = features.shape
    tokens = rows * n_slow * n_fast
    total_rows = n_cfg * n_x * n_core * tokens

    packed = packed_by_head(teacher_query[0, :, 0], teacher_key[0, :, 0], teacher_value[0, :, 0])
    heads = exchange(packed, ("cfg", "z", "y"))
    heads = heads.reshape(n_cfg, n_slow * n_fast, 3, rows, HDIM)

    scale = 1.0 + 0.5 * lax.dynamic_slice(guidance_index[:, 0], (cfg_index,), (1,)).astype(F32)
    time = (lax.dynamic_slice(timestep_index[:, 0], (cfg_index,), (1,)).astype(F32) + 0.5) / TSTEPS
    rank_index = jnp.arange(1, RANK + 1).astype(F32)
    modulation = 1.0 + 0.5 * jnp.cos(math.pi * rank_index * time + 0.25 * rank_index * scale)

    low = jnp.einsum("cl,elj->cej", features, adapter_down_weight, preferred_element_type=F32)
    low = (low * modulation).astype(BF).reshape(rows, 3 * RANK)
    low_slow = jnp.stack(from_each(low, "z"))

    groups = n_cfg * n_slow
    part_cols = width // (groups * n_fast)
    spread = parts_ahead(features.reshape(rows, groups, n_fast, part_cols), "y", 2)
    spread = [part.reshape(rows, groups * part_cols) for part in spread]
    columns = [spread[0]] + [shifted(spread[d], "y", d) for d in range(1, n_fast)]

    place = jnp.stack([lax.axis_index("z"), lax.axis_index("y")]).astype(jnp.int32)
    up = lax.dynamic_slice_in_dim(adapter_up_weight, seq_index * HDIM, HDIM, 2)
    inverse = jnp.full((1,), 1.0 / math.sqrt(total_rows), F32)

    heads, low_slow, up, place, *columns = lax.optimization_barrier(
        (heads, low_slow, up, place, *columns)
    )
    low_all = from_each(low_slow, "y")
    target = teacher(scale, heads)
    target, *low_all = lax.optimization_barrier((target, *low_all))
    out, upstream, student, stats = student_forward(place, inverse, heads, target, up, low_all)
    tokens_out = exchange(out.reshape(n_slow * n_fast, rows, HDIM), ("z", "y"))

    *back, up_partial = backward(place, student, upstream, stats, up, low_all)
    tokens_out, up_partial, *back = lax.optimization_barrier((tokens_out, up_partial, *back))
    student_out = jnp.moveaxis(tokens_out, 0, 1).reshape(rows, -1)

    back = summed_parts(back, "y").astype(BF)
    back = summed_parts([back[d] for d in range(n_slow)], "z")
    low_grad = (back.reshape(rows, 3, RANK) * modulation).astype(BF).reshape(rows, 3 * RANK)
    low_grads = jnp.concatenate(from_each(low_grad, "y"))
    down = dot(jnp.concatenate(columns), low_grads, TN).astype(BF)
    down = down.reshape(n_cfg, n_slow, n_x, n_core, -1, 3 * RANK).transpose(3, 2, 0, 1, 4, 5)
    down_rows, up_rows = down.shape[-2], RANK // (n_cfg * n_x * n_core)
    down = down.reshape(n_core, n_x, n_cfg, n_slow * down_rows, 3 * RANK)
    up_partial = up_partial.reshape(n_cfg, n_x, n_core, up_rows, 3 * HDIM).transpose(2, 1, 0, 3, 4)
    both = reduced(jnp.concatenate([down, up_partial], axis=3), ("core", "x", "cfg"))
    down, grad_up = both[: n_slow * down_rows], both[n_slow * down_rows :]
    grad_up = jnp.moveaxis(grad_up.reshape(up_rows, 3, HDIM), 1, 0)
    down = reduced(down.reshape(n_slow, down_rows, 3 * RANK), ("z",))
    grad_down = jnp.moveaxis(down.reshape(down_rows, 3, RANK), 1, 0)
    return student_out[None, None], grad_down, grad_up


def solution(mesh):
    sizes = {"cfg": 2, "z": 4, "y": 4, "x": 4, "core": 2}
    mesh = Mesh(mesh.devices.reshape(tuple(sizes.values())), tuple(sizes))
    seq, dp = ("z", "y"), ("x", "core")
    teacher = P("cfg", None, dp, seq, None)
    return jax.shard_map(
        body,
        mesh=mesh,
        in_specs=(
            teacher,
            teacher,
            teacher,
            P("cfg", dp, seq, None),
            P(),
            P(),
            P(None, dp),
            P(None, dp),
        ),
        out_specs=(
            P("cfg", dp, seq, None),
            P(None, ("cfg", *seq, *dp), None),
            P(None, ("cfg", *dp), seq),
        ),
        check_vma=False,
    )
```

```python
import functools
import math

import jax
import jax.numpy as jnp
from jax import lax
from jax.experimental import pallas as pl
from jax.experimental.pallas import tpu as pltpu
from jax.sharding import Mesh
from jax.sharding import PartitionSpec as P

HDIM = 128
RANK = 128
TSTEPS = 1000
FACTOR = HDIM ** (-0.5)
LOG2E = math.log2(math.e)
SCALE2 = FACTOR * LOG2E
BF = jnp.bfloat16
F32 = jnp.float32
NT = (((1,), (1,)), ((), ()))
TN = (((0,), (0,)), ((), ()))
MIB = 1 << 20


def dot(a, b, dims=(((1,), (0,)), ((), ()))):
    return lax.dot_general(a, b, dims, preferred_element_type=F32)


def exchange(value, axes):
    return lax.all_to_all(value, axes, split_axis=0, concat_axis=0, tiled=True)


def shifted(value, axis, distance):
    size = lax.axis_size(axis)
    return lax.ppermute(value, axis, [(i, (i + distance) % size) for i in range(size)])


def from_each(value, axis):
    return [value] + [shifted(value, axis, d) for d in range(1, lax.axis_size(axis))]


def summed_parts(parts, axis):
    total = parts[0].astype(F32)
    for d in range(1, lax.axis_size(axis)):
        total = total + shifted(parts[d].astype(BF), axis, d).astype(F32)
    return total


def parts_ahead(value, axis, dim):
    size, here = lax.axis_size(axis), lax.axis_index(axis)
    return [
        lax.dynamic_index_in_dim(value, (here + d) % size, dim, keepdims=False)
        for d in range(size)
    ]


def reduced(value, axes):
    for axis in axes:
        value = summed_parts(parts_ahead(value, axis, 0), axis)
    return value


def whole(shape):
    return pl.BlockSpec(shape, lambda i: (0,) * len(shape))


HBM = pl.BlockSpec(memory_space=pltpu.HBM)


def kept(arrays):
    return [pltpu.with_memory_space_constraint(array, pltpu.HBM) for array in arrays]


def started(source, target, semaphore):
    copy = pltpu.make_async_copy(source, target, semaphore)
    copy.start()
    return copy


def pack_kernel(q_ref, k_ref, v_ref, out_ref):
    heads = out_ref.shape[0]
    for part, ref in enumerate((q_ref, k_ref, v_ref)):
        for head in range(heads):
            out_ref[head, part] = ref[0, :, head * HDIM : (head + 1) * HDIM]


def packed_by_head(q, k, v):
    halves, rows, columns = q.shape
    heads = columns // HDIM
    step_rows = rows // 4
    spec = pl.BlockSpec((1, step_rows, columns), lambda i, j: (i, j, 0))
    return pl.pallas_call(
        pack_kernel,
        grid=(halves, rows // step_rows),
        in_specs=[spec] * 3,
        out_specs=pl.BlockSpec((heads, 3, step_rows, HDIM), lambda i, j: (i, 0, j, 0)),
        out_shape=jax.ShapeDtypeStruct((halves * heads, 3, rows, HDIM), q.dtype),
        cost_estimate=pl.CostEstimate(flops=0, transcendentals=0, bytes_accessed=12 * q.size),
        name="pack_heads",
    )(q, k, v)


def with_ones(ref, values):
    ref[:, :HDIM] = values
    ref[:, HDIM:] = jnp.ones_like(values)


def attended_rows(scores, value_ref):
    highest = jnp.max(scores, axis=-1, keepdims=True)
    raised = jnp.exp2((scores - highest) * SCALE2).astype(BF)
    both = dot(raised, value_ref[...])
    total = both[:, HDIM:]
    return both[:, :HDIM] / total, highest, total


def teacher_kernel(scale_ref, heads_ref, target_ref, query_ref, key_ref, value_ref, scores_ref):
    blocks, rows = heads_ref.shape[1], heads_ref.shape[3]
    tokens = blocks * rows
    scale = scale_ref[0]
    for one in range(2):
        for block in range(blocks):
            where = slice(block * rows, (block + 1) * rows)
            query_ref[one, where] = heads_ref[one, block, 0]
            key_ref[one, :, where] = jnp.transpose(heads_ref[one, block, 1])
            with_ones(value_ref.at[one, where], heads_ref[one, block, 2])
    step_rows = scores_ref.shape[1]
    steps = tokens // step_rows

    def rows_of(step):
        return pl.ds(pl.multiple_of(step * step_rows, step_rows), step_rows)

    def put_scores(step, one):
        scores_ref[one] = dot(query_ref[one, rows_of(step)], key_ref[one])

    def rounded(one):
        return attended_rows(scores_ref[one], value_ref.at[one])[0].astype(BF).astype(F32)

    def one_block(step, carry):
        put_scores(step, 1)
        conditional = rounded(0)
        put_scores(jnp.minimum(step + 1, steps - 1), 0)
        unconditional = rounded(1)
        target_ref[rows_of(step)] = unconditional + scale * (conditional - unconditional)
        return carry

    put_scores(0, 0)
    lax.fori_loop(0, steps, one_block, 0)


def teacher(scale, heads):
    tokens = heads.shape[1] * heads.shape[3]
    return pl.pallas_call(
        teacher_kernel,
        grid=(1,),
        in_specs=[pl.BlockSpec(memory_space=pltpu.SMEM), whole(heads.shape)],
        out_specs=whole((tokens, HDIM)),
        out_shape=jax.ShapeDtypeStruct((tokens, HDIM), F32),
        scratch_shapes=[
            pltpu.VMEM((2, tokens, HDIM), BF),
            pltpu.VMEM((2, HDIM, tokens), BF),
            pltpu.VMEM((2, tokens, 2 * HDIM), BF),
            pltpu.VMEM((2, 256, tokens), F32),
        ],
        cost_estimate=pl.CostEstimate(
            flops=8 * tokens * tokens * HDIM,
            transcendentals=2 * tokens * tokens,
            bytes_accessed=4 * MIB,
        ),
        compiler_params=pltpu.CompilerParams(vmem_limit_bytes=48 * MIB),
        name="teacher_forward",
    )(scale, heads)


def student_kernel(n_fast, place_ref, inv_ref, heads_ref, target_ref, up_ref, *refs):
    low_refs = refs[:n_fast]
    outs, locals_ = refs[n_fast : n_fast + 4], refs[n_fast + 4 : n_fast + 8]
    out_ref, upstream_ref, student_ref, stats_ref = locals_
    key_ref, value_ref, scores_ref, sems = refs[n_fast + 8 :]
    rows = heads_ref.shape[3]
    tokens = out_ref.shape[0]
    n_slow = low_refs[0].shape[0]
    here_slow, here_fast = place_ref[0], place_ref[1]
    inverse = inv_ref[0]

    for part in range(3):
        up = up_ref[part]
        for fast in range(n_fast):
            low = low_refs[fast][:, :, part * RANK : (part + 1) * RANK]
            adapted = dot(low.reshape(n_slow * rows, RANK), up)
            for slow in range(n_slow):
                block = lax.rem(here_slow - slow + n_slow, n_slow) * n_fast + lax.rem(
                    here_fast - fast + n_fast, n_fast
                )
                frozen = heads_ref[0, block, part].astype(F32)
                where = pl.ds(pl.multiple_of(block * rows, rows), rows)
                student_ref[part, where] = (
                    frozen + adapted[slow * rows : (slow + 1) * rows]
                ).astype(BF)
    copies = [started(student_ref, outs[2], sems.at[2])]
    for block in range(n_slow * n_fast):
        where = slice(block * rows, (block + 1) * rows)
        key_ref[:, where] = jnp.transpose(student_ref[1, where])
        with_ones(value_ref.at[where], student_ref[2, where])
    step_rows = scores_ref.shape[1]
    steps = tokens // step_rows

    def rows_of(step):
        return pl.ds(pl.multiple_of(step * step_rows, step_rows), step_rows)

    def put_scores(step, slot):
        scores_ref[slot] = dot(student_ref[0, rows_of(step)], key_ref[...])

    def finish(step, slot):
        here = rows_of(step)
        attended, highest, total = attended_rows(scores_ref[slot], value_ref)
        rounded = attended.astype(BF)
        out_ref[here] = rounded
        upstream = ((rounded.astype(F32) - target_ref[here]) * inverse).astype(BF)
        upstream_ref[here] = upstream
        level = highest * SCALE2 + jnp.log2(total)
        center = jnp.sum(attended * upstream.astype(F32), axis=-1, keepdims=True)
        stats_ref[0:1, here] = jnp.transpose(level)[0:1]
        stats_ref[1:2, here] = jnp.transpose(jnp.broadcast_to(center, (step_rows, HDIM)))[0:1]

    def two_blocks(pair, carry):
        put_scores(2 * pair + 1, 1)
        finish(2 * pair, 0)
        put_scores(jnp.minimum(2 * pair + 2, steps - 1), 0)
        finish(2 * pair + 1, 1)
        return carry

    stats_ref[...] = jnp.zeros_like(stats_ref)
    put_scores(0, 0)
    lax.fori_loop(0, steps // 2, two_blocks, 0)
    copies += [started(locals_[i], outs[i], sems.at[i]) for i in (0, 1, 3)]
    for copy in copies:
        copy.wait()


def student_forward(place, inverse, heads, target, up, low):
    tokens = target.shape[0]
    one_pass = (1, *heads.shape[1:])
    smem = pl.BlockSpec(memory_space=pltpu.SMEM)
    outs = [
        jax.ShapeDtypeStruct((tokens, HDIM), BF),
        jax.ShapeDtypeStruct((tokens, HDIM), BF),
        jax.ShapeDtypeStruct((3, tokens, HDIM), BF),
        jax.ShapeDtypeStruct((8, tokens), F32),
    ]
    return pl.pallas_call(
        functools.partial(student_kernel, len(low)),
        grid=(1,),
        in_specs=[smem, smem, whole(one_pass)]
        + [whole(operand.shape) for operand in (target, up, *low)],
        out_specs=[HBM] * len(outs),
        out_shape=[pltpu.HBM(out.shape, out.dtype) for out in outs],
        scratch_shapes=[pltpu.VMEM(out.shape, out.dtype) for out in outs]
        + [
            pltpu.VMEM((HDIM, tokens), BF),
            pltpu.VMEM((tokens, 2 * HDIM), BF),
            pltpu.VMEM((2, 256, tokens), F32),
            pltpu.SemaphoreType.DMA((len(outs),)),
        ],
        cost_estimate=pl.CostEstimate(
            flops=4 * tokens * tokens * HDIM,
            transcendentals=tokens * tokens,
            bytes_accessed=6 * MIB,
        ),
        compiler_params=pltpu.CompilerParams(vmem_limit_bytes=48 * MIB),
        name="student_forward",
    )(place, inverse, heads, target, up, *low)


def backward_kernel(n_fast, place_ref, up_ref, *refs):
    n_in = n_fast + 3
    sources, outs, refs = refs[:n_in], refs[n_in : n_in + n_fast + 1], refs[n_in + n_fast + 1 :]
    student_ref, upstream_ref, stats_ref, low_ref, back_ref, grad_up_ref = refs[:6]
    dq_ref, dk_ref, dv_ref, flat_ref, in_sems, out_sems = refs[6:]
    _, n_slow, rows, _ = low_ref.shape
    tokens = student_ref.shape[1]
    here_slow, here_fast = place_ref[0], place_ref[1]
    targets = [student_ref, upstream_ref, stats_ref] + [low_ref.at[d] for d in range(n_fast)]
    loads = [started(sources[i], targets[i], in_sems.at[i]) for i in range(n_in)]
    for load in loads[:3]:
        load.wait()
    step_rows = 512
    dk_ref[...] = jnp.zeros_like(dk_ref)
    dv_ref[...] = jnp.zeros_like(dv_ref)
    flat_ref[...] = jnp.transpose(student_ref[1])

    def one_block(step, carry):
        here = pl.ds(pl.multiple_of(step * step_rows, step_rows), step_rows)
        query = student_ref[0, here]
        upstream = upstream_ref[here]
        level = stats_ref[0:1, here]
        center = stats_ref[1:2, here]
        prob = jnp.exp2(dot(student_ref[1], query, NT) * SCALE2 - level)
        dv_ref[...] += dot(prob.astype(BF), upstream)
        dprob = dot(student_ref[2], upstream, NT)
        dscore = (prob * (dprob - center)).astype(BF)
        dk_ref[...] += dot(dscore, query)
        dq_ref[here] = jnp.transpose(dot(flat_ref[...], dscore))
        return carry

    lax.fori_loop(0, tokens // step_rows, one_block, 0)
    for load in loads[3:]:
        load.wait()

    def grads(ref, factor, slow, fast):
        block = lax.rem(here_slow + slow, n_slow) * n_fast + lax.rem(here_fast + fast, n_fast)
        grad = ref[pl.ds(pl.multiple_of(block * rows, rows), rows)] * factor
        return grad.astype(BF)

    parts = ((dq_ref, FACTOR), (dk_ref, FACTOR), (dv_ref, 1.0))
    stores = []
    for fast in (*range(1, n_fast), 0):
        for part, (ref, factor) in enumerate(parts):
            columns = slice(part * RANK, (part + 1) * RANK)
            for slow in range(n_slow):
                grad = grads(ref, factor, slow, fast)
                back_ref[fast, slow, :, columns] = dot(grad, up_ref[part], NT).astype(BF)
        stores.append(started(back_ref.at[fast], outs[fast], out_sems.at[fast]))
    for part, (ref, factor) in enumerate(parts):
        columns = slice(part * RANK, (part + 1) * RANK)
        total = jnp.zeros((RANK, HDIM), F32)
        for fast in range(n_fast):
            for slow in range(n_slow):
                grad = grads(ref, factor, n_slow - slow, n_fast - fast)
                total += dot(low_ref[fast, slow, :, columns], grad, TN)
        grad_up_ref[:, part * HDIM : (part + 1) * HDIM] = total.astype(BF)
    stores.append(started(grad_up_ref, outs[n_fast], out_sems.at[n_fast]))
    for store in stores:
        store.wait()


def backward(place, student, upstream, stats, up, low):
    tokens, n_fast = student.shape[1], len(low)
    outs = [jax.ShapeDtypeStruct(low[0].shape, BF)] * n_fast
    outs.append(jax.ShapeDtypeStruct((RANK, 3 * HDIM), BF))
    return pl.pallas_call(
        functools.partial(backward_kernel, n_fast),
        grid=(1,),
        in_specs=[pl.BlockSpec(memory_space=pltpu.SMEM), whole(up.shape)] + [HBM] * (n_fast + 3),
        out_specs=[HBM] * len(outs),
        out_shape=[pltpu.HBM(out.shape, out.dtype) for out in outs],
        scratch_shapes=[
            pltpu.VMEM(student.shape, BF),
            pltpu.VMEM(upstream.shape, BF),
            pltpu.VMEM(stats.shape, F32),
            pltpu.VMEM((n_fast, *low[0].shape), BF),
            pltpu.VMEM((n_fast, *low[0].shape), BF),
            pltpu.VMEM((RANK, 3 * HDIM), BF),
            *[pltpu.VMEM((tokens, HDIM), F32)] * 3,
            pltpu.VMEM((HDIM, tokens), BF),
            pltpu.SemaphoreType.DMA((n_fast + 3,)),
            pltpu.SemaphoreType.DMA((n_fast + 1,)),
        ],
        cost_estimate=pl.CostEstimate(
            flops=10 * tokens * tokens * HDIM,
            transcendentals=tokens * tokens,
            bytes_accessed=6 * MIB,
        ),
        compiler_params=pltpu.CompilerParams(vmem_limit_bytes=48 * MIB),
        name="attention_backward",
    )(place, up, *kept((student, upstream, stats, *low)))


def body(
    teacher_query,
    teacher_key,
    teacher_value,
    hidden,
    adapter_down_weight,
    adapter_up_weight,
    guidance_index,
    timestep_index,
):
    n_cfg, n_slow, n_fast = (lax.axis_size(a) for a in ("cfg", "z", "y"))
    n_x, n_core = (lax.axis_size(a) for a in ("x", "core"))
    cfg_index = lax.axis_index("cfg")
    seq_index = lax.axis_index(("z", "y"))
    features = hidden[0, 0]
    rows, width = features.shape
    tokens = rows * n_slow * n_fast
    total_rows = n_cfg * n_x * n_core * tokens

    packed = packed_by_head(teacher_query[0, :, 0], teacher_key[0, :, 0], teacher_value[0, :, 0])
    heads = exchange(packed, ("cfg", "z", "y"))
    heads = heads.reshape(n_cfg, n_slow * n_fast, 3, rows, HDIM)

    scale = 1.0 + 0.5 * lax.dynamic_slice(guidance_index[:, 0], (cfg_index,), (1,)).astype(F32)
    time = (lax.dynamic_slice(timestep_index[:, 0], (cfg_index,), (1,)).astype(F32) + 0.5) / TSTEPS
    rank_index = jnp.arange(1, RANK + 1).astype(F32)
    modulation = 1.0 + 0.5 * jnp.cos(math.pi * rank_index * time + 0.25 * rank_index * scale)

    low = jnp.einsum("cl,elj->cej", features, adapter_down_weight, preferred_element_type=F32)
    low = (low * modulation).astype(BF).reshape(rows, 3 * RANK)
    low_slow = jnp.stack(from_each(low, "z"))

    groups = n_cfg * n_slow
    part_cols = width // (groups * n_fast)
    spread = parts_ahead(features.reshape(rows, groups, n_fast, part_cols), "y", 2)
    spread = [part.reshape(rows, groups * part_cols) for part in spread]
    columns = [spread[0]] + [shifted(spread[d], "y", d) for d in range(1, n_fast - 1)]
    spread = spread[-1]

    place = jnp.stack([lax.axis_index("z"), lax.axis_index("y")]).astype(jnp.int32)
    up = lax.dynamic_slice_in_dim(adapter_up_weight, seq_index * HDIM, HDIM, 2)
    inverse = jnp.full((1,), 1.0 / math.sqrt(total_rows), F32)

    heads, low_slow, up, place, spread, *columns = lax.optimization_barrier(
        (heads, low_slow, up, place, spread, *columns)
    )
    low_all = from_each(low_slow, "y")
    target = teacher(scale, heads)
    target, *low_all = lax.optimization_barrier((target, *low_all))
    out, upstream, student, stats = student_forward(place, inverse, heads, target, up, low_all)
    tokens_out = exchange(out.reshape(n_slow * n_fast, rows, HDIM), ("z", "y"))

    *back, up_partial = backward(place, student, upstream, stats, up, low_all)
    tokens_out, up_partial, spread, *back = lax.optimization_barrier(
        (tokens_out, up_partial, spread, *back)
    )
    columns.append(shifted(spread, "y", n_fast - 1))
    student_out = jnp.moveaxis(tokens_out, 0, 1).reshape(rows, -1)

    back = summed_parts(back, "y").astype(BF)
    back = summed_parts([back[d] for d in range(n_slow)], "z")
    low_grad = (back.reshape(rows, 3, RANK) * modulation).astype(BF).reshape(rows, 3 * RANK)
    low_grads = jnp.concatenate(from_each(low_grad, "y"))
    down = dot(jnp.concatenate(columns), low_grads, TN).astype(BF)
    down = down.reshape(n_cfg, n_slow, n_x, n_core, -1, 3 * RANK).transpose(3, 2, 0, 1, 4, 5)
    down_rows, up_rows = down.shape[-2], RANK // (n_cfg * n_x * n_core)
    down = down.reshape(n_core, n_x, n_cfg, n_slow * down_rows, 3 * RANK)
    up_partial = up_partial.reshape(n_cfg, n_x, n_core, up_rows, 3 * HDIM).transpose(2, 1, 0, 3, 4)
    both = reduced(jnp.concatenate([down, up_partial], axis=3), ("core", "x", "cfg"))
    down, grad_up = both[: n_slow * down_rows], both[n_slow * down_rows :]
    grad_up = jnp.moveaxis(grad_up.reshape(up_rows, 3, HDIM), 1, 0)
    down = reduced(down.reshape(n_slow, down_rows, 3 * RANK), ("z",))
    grad_down = jnp.moveaxis(down.reshape(down_rows, 3, RANK), 1, 0)
    return student_out[None, None], grad_down, grad_up


def solution(mesh):
    sizes = {"cfg": 2, "z": 4, "y": 4, "x": 4, "core": 2}
    mesh = Mesh(mesh.devices.reshape(tuple(sizes.values())), tuple(sizes))
    seq, dp = ("z", "y"), ("x", "core")
    teacher = P("cfg", None, dp, seq, None)
    return jax.shard_map(
        body,
        mesh=mesh,
        in_specs=(
            teacher,
            teacher,
            teacher,
            P("cfg", dp, seq, None),
            P(),
            P(),
            P(None, dp),
            P(None, dp),
        ),
        out_specs=(
            P("cfg", dp, seq, None),
            P(None, ("cfg", *seq, *dp), None),
            P(None, ("cfg", *dp), seq),
        ),
        check_vma=False,
    )
```

```python
import functools
import math

import jax
import jax.numpy as jnp
from jax import lax
from jax.experimental import pallas as pl
from jax.experimental.pallas import tpu as pltpu
from jax.sharding import Mesh
from jax.sharding import PartitionSpec as P

HDIM = 128
RANK = 128
TSTEPS = 1000
FACTOR = HDIM ** (-0.5)
LOG2E = math.log2(math.e)
SCALE2 = FACTOR * LOG2E
BF = jnp.bfloat16
F32 = jnp.float32
NT = (((1,), (1,)), ((), ()))
TN = (((0,), (0,)), ((), ()))
MIB = 1 << 20


def dot(a, b, dims=(((1,), (0,)), ((), ()))):
    return lax.dot_general(a, b, dims, preferred_element_type=F32)


def exchange(value, axes):
    return lax.all_to_all(value, axes, split_axis=0, concat_axis=0, tiled=True)


def shifted(value, axis, distance):
    size = lax.axis_size(axis)
    return lax.ppermute(value, axis, [(i, (i + distance) % size) for i in range(size)])


def from_each(value, axis):
    return [value] + [shifted(value, axis, d) for d in range(1, lax.axis_size(axis))]


def summed_parts(parts, axis):
    total = parts[0].astype(F32)
    for d in range(1, lax.axis_size(axis)):
        total = total + shifted(parts[d].astype(BF), axis, d).astype(F32)
    return total


def parts_ahead(value, axis, dim):
    size, here = lax.axis_size(axis), lax.axis_index(axis)
    return [
        lax.dynamic_index_in_dim(value, (here + d) % size, dim, keepdims=False)
        for d in range(size)
    ]


def reduced(value, axes):
    for axis in axes:
        value = summed_parts(parts_ahead(value, axis, 0), axis)
    return value


def whole(shape):
    return pl.BlockSpec(shape, lambda i: (0,) * len(shape))


HBM = pl.BlockSpec(memory_space=pltpu.HBM)


def kept(arrays):
    return [pltpu.with_memory_space_constraint(array, pltpu.HBM) for array in arrays]


def started(source, target, semaphore):
    copy = pltpu.make_async_copy(source, target, semaphore)
    copy.start()
    return copy


def pack_kernel(q_ref, k_ref, v_ref, out_ref):
    heads = out_ref.shape[0]
    for part, ref in enumerate((q_ref, k_ref, v_ref)):
        for head in range(heads):
            out_ref[head, part] = ref[0, :, head * HDIM : (head + 1) * HDIM]


def packed_by_head(q, k, v):
    halves, rows, columns = q.shape
    heads = columns // HDIM
    spec = pl.BlockSpec((1, rows, columns), lambda i: (i, 0, 0))
    return pl.pallas_call(
        pack_kernel,
        grid=(halves,),
        in_specs=[spec] * 3,
        out_specs=pl.BlockSpec((heads, 3, rows, HDIM), lambda i: (i, 0, 0, 0)),
        out_shape=jax.ShapeDtypeStruct((halves * heads, 3, rows, HDIM), q.dtype),
        cost_estimate=pl.CostEstimate(flops=0, transcendentals=0, bytes_accessed=12 * q.size),
        name="pack_heads",
    )(q, k, v)


def with_ones(ref, values):
    ref[:, :HDIM] = values
    ref[:, HDIM:] = jnp.ones_like(values)


def attended_rows(scores, value_ref):
    highest = jnp.max(scores, axis=-1, keepdims=True)
    raised = jnp.exp2((scores - highest) * SCALE2).astype(BF)
    both = dot(raised, value_ref[...])
    total = both[:, HDIM:]
    return both[:, :HDIM] / total, highest, total


def teacher_kernel(scale_ref, heads_ref, target_ref, query_ref, key_ref, value_ref, scores_ref):
    blocks, rows = heads_ref.shape[1], heads_ref.shape[3]
    tokens = blocks * rows
    scale = scale_ref[0]
    for one in range(2):
        for block in range(blocks):
            where = slice(block * rows, (block + 1) * rows)
            query_ref[one, where] = heads_ref[one, block, 0]
            key_ref[one, :, where] = jnp.transpose(heads_ref[one, block, 1])
            with_ones(value_ref.at[one, where], heads_ref[one, block, 2])
    step_rows = scores_ref.shape[1]
    steps = tokens // step_rows

    def rows_of(step):
        return pl.ds(pl.multiple_of(step * step_rows, step_rows), step_rows)

    def put_scores(step, one):
        scores_ref[one] = dot(query_ref[one, rows_of(step)], key_ref[one])

    def rounded(one):
        return attended_rows(scores_ref[one], value_ref.at[one])[0].astype(BF).astype(F32)

    def one_block(step, carry):
        put_scores(step, 1)
        conditional = rounded(0)
        put_scores(jnp.minimum(step + 1, steps - 1), 0)
        unconditional = rounded(1)
        target_ref[rows_of(step)] = unconditional + scale * (conditional - unconditional)
        return carry

    put_scores(0, 0)
    lax.fori_loop(0, steps, one_block, 0)


def teacher(scale, heads):
    tokens = heads.shape[1] * heads.shape[3]
    return pl.pallas_call(
        teacher_kernel,
        grid=(1,),
        in_specs=[pl.BlockSpec(memory_space=pltpu.SMEM), whole(heads.shape)],
        out_specs=whole((tokens, HDIM)),
        out_shape=jax.ShapeDtypeStruct((tokens, HDIM), F32),
        scratch_shapes=[
            pltpu.VMEM((2, tokens, HDIM), BF),
            pltpu.VMEM((2, HDIM, tokens), BF),
            pltpu.VMEM((2, tokens, 2 * HDIM), BF),
            pltpu.VMEM((2, 256, tokens), F32),
        ],
        cost_estimate=pl.CostEstimate(
            flops=8 * tokens * tokens * HDIM,
            transcendentals=2 * tokens * tokens,
            bytes_accessed=4 * MIB,
        ),
        compiler_params=pltpu.CompilerParams(vmem_limit_bytes=48 * MIB),
        name="teacher_forward",
    )(scale, heads)


def student_kernel(n_fast, place_ref, inv_ref, heads_ref, target_ref, up_ref, *refs):
    low_refs = refs[:n_fast]
    outs, locals_ = refs[n_fast : n_fast + 4], refs[n_fast + 4 : n_fast + 8]
    out_ref, upstream_ref, student_ref, stats_ref = locals_
    key_ref, value_ref, scores_ref, sems = refs[n_fast + 8 :]
    rows = heads_ref.shape[3]
    tokens = out_ref.shape[0]
    n_slow = low_refs[0].shape[0]
    here_slow, here_fast = place_ref[0], place_ref[1]
    inverse = inv_ref[0]

    for part in range(3):
        up = up_ref[part]
        for fast in range(n_fast):
            low = low_refs[fast][:, :, part * RANK : (part + 1) * RANK]
            adapted = dot(low.reshape(n_slow * rows, RANK), up)
            for slow in range(n_slow):
                block = lax.rem(here_slow - slow + n_slow, n_slow) * n_fast + lax.rem(
                    here_fast - fast + n_fast, n_fast
                )
                frozen = heads_ref[0, block, part].astype(F32)
                where = pl.ds(pl.multiple_of(block * rows, rows), rows)
                student_ref[part, where] = (
                    frozen + adapted[slow * rows : (slow + 1) * rows]
                ).astype(BF)
    copies = [started(student_ref, outs[2], sems.at[2])]
    for block in range(n_slow * n_fast):
        where = slice(block * rows, (block + 1) * rows)
        key_ref[:, where] = jnp.transpose(student_ref[1, where])
        with_ones(value_ref.at[where], student_ref[2, where])
    step_rows = scores_ref.shape[1]
    steps = tokens // step_rows

    def rows_of(step):
        return pl.ds(pl.multiple_of(step * step_rows, step_rows), step_rows)

    def put_scores(step, slot):
        scores_ref[slot] = dot(student_ref[0, rows_of(step)], key_ref[...])

    def finish(step, slot):
        here = rows_of(step)
        attended, highest, total = attended_rows(scores_ref[slot], value_ref)
        rounded = attended.astype(BF)
        out_ref[here] = rounded
        upstream = ((rounded.astype(F32) - target_ref[here]) * inverse).astype(BF)
        upstream_ref[here] = upstream
        level = highest * SCALE2 + jnp.log2(total)
        center = jnp.sum(attended * upstream.astype(F32), axis=-1, keepdims=True)
        stats_ref[0:1, here] = jnp.transpose(level)[0:1]
        stats_ref[1:2, here] = jnp.transpose(jnp.broadcast_to(center, (step_rows, HDIM)))[0:1]

    def two_blocks(pair, carry):
        put_scores(2 * pair + 1, 1)
        finish(2 * pair, 0)
        put_scores(jnp.minimum(2 * pair + 2, steps - 1), 0)
        finish(2 * pair + 1, 1)
        return carry

    stats_ref[...] = jnp.zeros_like(stats_ref)
    put_scores(0, 0)
    lax.fori_loop(0, steps // 2, two_blocks, 0)
    copies += [started(locals_[i], outs[i], sems.at[i]) for i in (0, 1, 3)]
    for copy in copies:
        copy.wait()


def student_forward(place, inverse, heads, target, up, low):
    tokens = target.shape[0]
    one_pass = (1, *heads.shape[1:])
    smem = pl.BlockSpec(memory_space=pltpu.SMEM)
    outs = [
        jax.ShapeDtypeStruct((tokens, HDIM), BF),
        jax.ShapeDtypeStruct((tokens, HDIM), BF),
        jax.ShapeDtypeStruct((3, tokens, HDIM), BF),
        jax.ShapeDtypeStruct((8, tokens), F32),
    ]
    return pl.pallas_call(
        functools.partial(student_kernel, len(low)),
        grid=(1,),
        in_specs=[smem, smem, whole(one_pass)]
        + [whole(operand.shape) for operand in (target, up, *low)],
        out_specs=[HBM] * len(outs),
        out_shape=[pltpu.HBM(out.shape, out.dtype) for out in outs],
        scratch_shapes=[pltpu.VMEM(out.shape, out.dtype) for out in outs]
        + [
            pltpu.VMEM((HDIM, tokens), BF),
            pltpu.VMEM((tokens, 2 * HDIM), BF),
            pltpu.VMEM((2, 256, tokens), F32),
            pltpu.SemaphoreType.DMA((len(outs),)),
        ],
        cost_estimate=pl.CostEstimate(
            flops=4 * tokens * tokens * HDIM,
            transcendentals=tokens * tokens,
            bytes_accessed=6 * MIB,
        ),
        compiler_params=pltpu.CompilerParams(vmem_limit_bytes=48 * MIB),
        name="student_forward",
    )(place, inverse, heads, target, up, *low)


def backward_kernel(n_fast, place_ref, up_ref, *refs):
    n_in = n_fast + 3
    sources, outs, refs = refs[:n_in], refs[n_in : n_in + n_fast], refs[n_in + n_fast :]
    grad_up_ref, student_ref, upstream_ref, stats_ref, low_ref, back_ref = refs[:6]
    dq_ref, dk_ref, dv_ref, flat_ref, in_sems, out_sems = refs[6:]
    _, n_slow, rows, _ = low_ref.shape
    tokens = student_ref.shape[1]
    here_slow, here_fast = place_ref[0], place_ref[1]
    targets = [student_ref, upstream_ref, stats_ref] + [low_ref.at[d] for d in range(n_fast)]
    loads = [started(sources[i], targets[i], in_sems.at[i]) for i in range(n_in)]
    for load in loads[:3]:
        load.wait()
    step_rows = 512
    dk_ref[...] = jnp.zeros_like(dk_ref)
    dv_ref[...] = jnp.zeros_like(dv_ref)
    flat_ref[...] = jnp.transpose(student_ref[1])

    def one_block(step, carry):
        here = pl.ds(pl.multiple_of(step * step_rows, step_rows), step_rows)
        query = student_ref[0, here]
        upstream = upstream_ref[here]
        level = stats_ref[0:1, here]
        center = stats_ref[1:2, here]
        prob = jnp.exp2(dot(student_ref[1], query, NT) * SCALE2 - level)
        dv_ref[...] += dot(prob.astype(BF), upstream)
        dprob = dot(student_ref[2], upstream, NT)
        dscore = (prob * (dprob - center)).astype(BF)
        dk_ref[...] += dot(dscore, query)
        dq_ref[here] = jnp.transpose(dot(flat_ref[...], dscore))
        return carry

    lax.fori_loop(0, tokens // step_rows, one_block, 0)
    for load in loads[3:]:
        load.wait()

    def grads(ref, factor, slow, fast):
        block = lax.rem(here_slow + slow, n_slow) * n_fast + lax.rem(here_fast + fast, n_fast)
        grad = ref[pl.ds(pl.multiple_of(block * rows, rows), rows)] * factor
        return grad.astype(BF)

    parts = ((dq_ref, FACTOR), (dk_ref, FACTOR), (dv_ref, 1.0))
    stores = []
    for fast in (*range(1, n_fast), 0):
        for part, (ref, factor) in enumerate(parts):
            columns = slice(part * RANK, (part + 1) * RANK)
            for slow in range(n_slow):
                grad = grads(ref, factor, slow, fast)
                back_ref[fast, slow, :, columns] = dot(grad, up_ref[part], NT).astype(BF)
        stores.append(started(back_ref.at[fast], outs[fast], out_sems.at[fast]))
    for part, (ref, factor) in enumerate(parts):
        columns = slice(part * RANK, (part + 1) * RANK)
        total = jnp.zeros((RANK, HDIM), F32)
        for fast in range(n_fast):
            for slow in range(n_slow):
                grad = grads(ref, factor, n_slow - slow, n_fast - fast)
                total += dot(low_ref[fast, slow, :, columns], grad, TN)
        grad_up_ref[:, part * HDIM : (part + 1) * HDIM] = total.astype(BF)
    for store in stores:
        store.wait()


def backward(place, student, upstream, stats, up, low):
    tokens, n_fast = student.shape[1], len(low)
    up_shape = (RANK, 3 * HDIM)
    return pl.pallas_call(
        functools.partial(backward_kernel, n_fast),
        grid=(1,),
        in_specs=[pl.BlockSpec(memory_space=pltpu.SMEM), whole(up.shape)] + [HBM] * (n_fast + 3),
        out_specs=[HBM] * n_fast + [whole(up_shape)],
        out_shape=[pltpu.HBM(low[0].shape, BF)] * n_fast + [jax.ShapeDtypeStruct(up_shape, BF)],
        scratch_shapes=[
            pltpu.VMEM(student.shape, BF),
            pltpu.VMEM(upstream.shape, BF),
            pltpu.VMEM(stats.shape, F32),
            pltpu.VMEM((n_fast, *low[0].shape), BF),
            pltpu.VMEM((n_fast, *low[0].shape), BF),
            *[pltpu.VMEM((tokens, HDIM), F32)] * 3,
            pltpu.VMEM((HDIM, tokens), BF),
            pltpu.SemaphoreType.DMA((n_fast + 3,)),
            pltpu.SemaphoreType.DMA((n_fast,)),
        ],
        cost_estimate=pl.CostEstimate(
            flops=10 * tokens * tokens * HDIM,
            transcendentals=tokens * tokens,
            bytes_accessed=6 * MIB,
        ),
        compiler_params=pltpu.CompilerParams(vmem_limit_bytes=48 * MIB),
        name="attention_backward",
    )(place, up, *kept((student, upstream, stats, *low)))


def body(
    teacher_query,
    teacher_key,
    teacher_value,
    hidden,
    adapter_down_weight,
    adapter_up_weight,
    guidance_index,
    timestep_index,
):
    n_cfg, n_slow, n_fast = (lax.axis_size(a) for a in ("cfg", "z", "y"))
    n_x, n_core = (lax.axis_size(a) for a in ("x", "core"))
    cfg_index = lax.axis_index("cfg")
    seq_index = lax.axis_index(("z", "y"))
    features = hidden[0, 0]
    rows, width = features.shape
    tokens = rows * n_slow * n_fast
    total_rows = n_cfg * n_x * n_core * tokens

    scale = 1.0 + 0.5 * lax.dynamic_slice(guidance_index[:, 0], (cfg_index,), (1,)).astype(F32)
    time = (lax.dynamic_slice(timestep_index[:, 0], (cfg_index,), (1,)).astype(F32) + 0.5) / TSTEPS
    rank_index = jnp.arange(1, RANK + 1).astype(F32)
    modulation = 1.0 + 0.5 * jnp.cos(math.pi * rank_index * time + 0.25 * rank_index * scale)

    low = [
        (dot(features, adapter_down_weight[part]) * modulation).astype(BF) for part in range(3)
    ]
    low = jnp.concatenate(low, axis=1)
    packed = packed_by_head(teacher_query[0, :, 0], teacher_key[0, :, 0], teacher_value[0, :, 0])
    low_parts = from_each(low, "z")
    packed, *low_parts = lax.optimization_barrier((packed, *low_parts))
    heads = exchange(packed, ("cfg", "z", "y"))
    heads = heads.reshape(n_cfg, n_slow * n_fast, 3, rows, HDIM)
    low_all = from_each(jnp.stack(low_parts), "y")

    groups = n_cfg * n_slow
    part_cols = width // (groups * n_fast)
    features, low_all[0] = lax.optimization_barrier((features, low_all[0]))
    spread = parts_ahead(features.reshape(rows, groups, n_fast, part_cols), "y", 2)
    spread = [part.reshape(rows, groups * part_cols) for part in spread]
    columns = [spread[0]] + [shifted(spread[d], "y", d) for d in range(1, n_fast - 1)]
    spread = spread[-1]

    place = jnp.stack([lax.axis_index("z"), lax.axis_index("y")]).astype(jnp.int32)
    up = lax.dynamic_slice_in_dim(adapter_up_weight, seq_index * HDIM, HDIM, 2)
    inverse = jnp.full((1,), 1.0 / math.sqrt(total_rows), F32)

    heads, up, place, spread, *columns = lax.optimization_barrier(
        (heads, up, place, spread, *columns)
    )
    target = teacher(scale, heads)
    target, *low_all = lax.optimization_barrier((target, *low_all))
    out, upstream, student, stats = student_forward(place, inverse, heads, target, up, low_all)
    tokens_out = exchange(out.reshape(n_slow * n_fast, rows, HDIM), ("z", "y"))

    *back, up_partial = backward(place, student, upstream, stats, up, low_all)
    tokens_out, up_partial, spread, *back = lax.optimization_barrier(
        (tokens_out, up_partial, spread, *back)
    )
    columns.append(shifted(spread, "y", n_fast - 1))
    student_out = jnp.moveaxis(tokens_out, 0, 1).reshape(rows, -1)

    back = summed_parts(back, "y").astype(BF)
    back = summed_parts([back[d] for d in range(n_slow)], "z")
    low_grad = (back.reshape(rows, 3, RANK) * modulation).astype(BF).reshape(rows, 3 * RANK)
    low_grads = jnp.concatenate(from_each(low_grad, "y"))
    down = dot(jnp.concatenate(columns), low_grads, TN).astype(BF)
    down = down.reshape(n_cfg, n_slow, n_x, n_core, -1, 3 * RANK).transpose(3, 2, 0, 1, 4, 5)
    down_rows, up_rows = down.shape[-2], RANK // (n_cfg * n_x * n_core)
    down = down.reshape(n_core, n_x, n_cfg, n_slow * down_rows, 3 * RANK)
    up_partial = up_partial.reshape(n_cfg, n_x, n_core, up_rows, 3 * HDIM).transpose(2, 1, 0, 3, 4)
    both = reduced(jnp.concatenate([down, up_partial], axis=3), ("core", "x", "cfg"))
    down, grad_up = both[: n_slow * down_rows], both[n_slow * down_rows :]
    grad_up = jnp.moveaxis(grad_up.reshape(up_rows, 3, HDIM), 1, 0)
    down = reduced(down.reshape(n_slow, down_rows, 3 * RANK), ("z",))
    grad_down = jnp.moveaxis(down.reshape(down_rows, 3, RANK), 1, 0)
    return student_out[None, None], grad_down, grad_up


def solution(mesh):
    sizes = {"cfg": 2, "z": 4, "y": 4, "x": 4, "core": 2}
    mesh = Mesh(mesh.devices.reshape(tuple(sizes.values())), tuple(sizes))
    seq, dp = ("z", "y"), ("x", "core")
    teacher = P("cfg", None, dp, seq, None)
    return jax.shard_map(
        body,
        mesh=mesh,
        in_specs=(
            teacher,
            teacher,
            teacher,
            P("cfg", dp, seq, None),
            P(),
            P(),
            P(None, dp),
            P(None, dp),
        ),
        out_specs=(
            P("cfg", dp, seq, None),
            P(None, ("cfg", *seq, *dp), None),
            P(None, ("cfg", *dp), seq),
        ),
        check_vma=False,
    )
```

```python
import functools
import math

import jax
import jax.numpy as jnp
from jax import lax
from jax.experimental import pallas as pl
from jax.experimental.pallas import tpu as pltpu
from jax.sharding import Mesh
from jax.sharding import PartitionSpec as P

HDIM = 128
RANK = 128
TSTEPS = 1000
FACTOR = HDIM ** (-0.5)
LOG2E = math.log2(math.e)
SCALE2 = FACTOR * LOG2E
BF = jnp.bfloat16
F32 = jnp.float32
NT = (((1,), (1,)), ((), ()))
TN = (((0,), (0,)), ((), ()))
MIB = 1 << 20


def dot(a, b, dims=(((1,), (0,)), ((), ()))):
    return lax.dot_general(a, b, dims, preferred_element_type=F32)


def exchange(value, axes):
    return lax.all_to_all(value, axes, split_axis=0, concat_axis=0, tiled=True)


def shifted(value, axis, distance):
    size = lax.axis_size(axis)
    return lax.ppermute(value, axis, [(i, (i + distance) % size) for i in range(size)])


def from_each(value, axis):
    return [value] + [shifted(value, axis, d) for d in range(1, lax.axis_size(axis))]


def summed_parts(parts, axis):
    total = parts[0].astype(F32)
    for d in range(1, lax.axis_size(axis)):
        total = total + shifted(parts[d].astype(BF), axis, d).astype(F32)
    return total


def parts_ahead(value, axis, dim):
    size, here = lax.axis_size(axis), lax.axis_index(axis)
    return [
        lax.dynamic_index_in_dim(value, (here + d) % size, dim, keepdims=False)
        for d in range(size)
    ]


def reduced(value, axes):
    for axis in axes:
        value = summed_parts(parts_ahead(value, axis, 0), axis)
    return value


def whole(shape):
    return pl.BlockSpec(shape, lambda i: (0,) * len(shape))


HBM = pl.BlockSpec(memory_space=pltpu.HBM)


def kept(arrays):
    return [pltpu.with_memory_space_constraint(array, pltpu.HBM) for array in arrays]


def started(source, target, semaphore):
    copy = pltpu.make_async_copy(source, target, semaphore)
    copy.start()
    return copy


def pack_kernel(q_ref, k_ref, v_ref, out_ref):
    heads = out_ref.shape[0]
    for part, ref in enumerate((q_ref, k_ref, v_ref)):
        for head in range(heads):
            out_ref[head, part] = ref[0, :, head * HDIM : (head + 1) * HDIM]


def packed_by_head(q, k, v):
    halves, rows, columns = q.shape
    heads = columns // HDIM
    spec = pl.BlockSpec((1, rows, columns), lambda i: (i, 0, 0))
    return pl.pallas_call(
        pack_kernel,
        grid=(halves,),
        in_specs=[spec] * 3,
        out_specs=pl.BlockSpec((heads, 3, rows, HDIM), lambda i: (i, 0, 0, 0)),
        out_shape=jax.ShapeDtypeStruct((halves * heads, 3, rows, HDIM), q.dtype),
        cost_estimate=pl.CostEstimate(flops=0, transcendentals=0, bytes_accessed=12 * q.size),
        name="pack_heads",
    )(q, k, v)


def with_ones(ref, values):
    ref[:, :HDIM] = values
    ref[:, HDIM:] = jnp.ones_like(values)


def attended_rows(scores, value_ref):
    highest = jnp.max(scores, axis=-1, keepdims=True)
    raised = jnp.exp2((scores - highest) * SCALE2).astype(BF)
    both = dot(raised, value_ref[...])
    total = both[:, HDIM:]
    return both[:, :HDIM] / total, highest, total


def teacher_kernel(scale_ref, heads_ref, target_ref, query_ref, key_ref, value_ref, scores_ref):
    blocks, rows = heads_ref.shape[1], heads_ref.shape[3]
    tokens = blocks * rows
    scale = scale_ref[0]
    for one in range(2):
        for block in range(blocks):
            where = slice(block * rows, (block + 1) * rows)
            query_ref[one, where] = heads_ref[one, block, 0]
            key_ref[one, :, where] = jnp.transpose(heads_ref[one, block, 1])
            with_ones(value_ref.at[one, where], heads_ref[one, block, 2])
    step_rows = scores_ref.shape[1]
    steps = tokens // step_rows

    def rows_of(step):
        return pl.ds(pl.multiple_of(step * step_rows, step_rows), step_rows)

    def put_scores(step, one):
        scores_ref[one] = dot(query_ref[one, rows_of(step)], key_ref[one])

    def rounded(one):
        return attended_rows(scores_ref[one], value_ref.at[one])[0].astype(BF).astype(F32)

    def one_block(step, carry):
        put_scores(step, 1)
        conditional = rounded(0)
        put_scores(jnp.minimum(step + 1, steps - 1), 0)
        unconditional = rounded(1)
        target_ref[rows_of(step)] = unconditional + scale * (conditional - unconditional)
        return carry

    put_scores(0, 0)
    lax.fori_loop(0, steps, one_block, 0)


def teacher(scale, heads):
    tokens = heads.shape[1] * heads.shape[3]
    return pl.pallas_call(
        teacher_kernel,
        grid=(1,),
        in_specs=[pl.BlockSpec(memory_space=pltpu.SMEM), whole(heads.shape)],
        out_specs=whole((tokens, HDIM)),
        out_shape=jax.ShapeDtypeStruct((tokens, HDIM), F32),
        scratch_shapes=[
            pltpu.VMEM((2, tokens, HDIM), BF),
            pltpu.VMEM((2, HDIM, tokens), BF),
            pltpu.VMEM((2, tokens, 2 * HDIM), BF),
            pltpu.VMEM((2, 256, tokens), F32),
        ],
        cost_estimate=pl.CostEstimate(
            flops=8 * tokens * tokens * HDIM,
            transcendentals=2 * tokens * tokens,
            bytes_accessed=4 * MIB,
        ),
        compiler_params=pltpu.CompilerParams(vmem_limit_bytes=48 * MIB),
        name="teacher_forward",
    )(scale, heads)


def student_kernel(n_fast, place_ref, inv_ref, heads_ref, target_ref, up_ref, *refs):
    low_refs = refs[:n_fast]
    outs, locals_ = refs[n_fast : n_fast + 4], refs[n_fast + 4 : n_fast + 8]
    out_ref, upstream_ref, student_ref, stats_ref = locals_
    key_ref, value_ref, scores_ref, sems = refs[n_fast + 8 :]
    rows = heads_ref.shape[3]
    tokens = out_ref.shape[0]
    n_slow = low_refs[0].shape[0]
    here_slow, here_fast = place_ref[0], place_ref[1]
    inverse = inv_ref[0]

    for part in range(3):
        up = up_ref[part]
        for fast in range(n_fast):
            low = low_refs[fast][:, :, part * RANK : (part + 1) * RANK]
            adapted = dot(low.reshape(n_slow * rows, RANK), up)
            for slow in range(n_slow):
                block = lax.rem(here_slow - slow + n_slow, n_slow) * n_fast + lax.rem(
                    here_fast - fast + n_fast, n_fast
                )
                frozen = heads_ref[0, block, part].astype(F32)
                where = pl.ds(pl.multiple_of(block * rows, rows), rows)
                student_ref[part, where] = (
                    frozen + adapted[slow * rows : (slow + 1) * rows]
                ).astype(BF)
    copies = [started(student_ref, outs[2], sems.at[2])]
    for block in range(n_slow * n_fast):
        where = slice(block * rows, (block + 1) * rows)
        key_ref[:, where] = jnp.transpose(student_ref[1, where])
        with_ones(value_ref.at[where], student_ref[2, where])
    step_rows = scores_ref.shape[1]
    steps = tokens // step_rows

    def rows_of(step):
        return pl.ds(pl.multiple_of(step * step_rows, step_rows), step_rows)

    def put_scores(step, slot):
        scores_ref[slot] = dot(student_ref[0, rows_of(step)], key_ref[...])

    def finish(step, slot):
        here = rows_of(step)
        attended, highest, total = attended_rows(scores_ref[slot], value_ref)
        rounded = attended.astype(BF)
        out_ref[here] = rounded
        upstream = ((rounded.astype(F32) - target_ref[here]) * inverse).astype(BF)
        upstream_ref[here] = upstream
        level = highest * SCALE2 + jnp.log2(total)
        center = jnp.sum(attended * upstream.astype(F32), axis=-1, keepdims=True)
        stats_ref[0:1, here] = jnp.transpose(level)[0:1]
        stats_ref[1:2, here] = jnp.transpose(jnp.broadcast_to(center, (step_rows, HDIM)))[0:1]

    def two_blocks(pair, carry):
        put_scores(2 * pair + 1, 1)
        finish(2 * pair, 0)
        put_scores(jnp.minimum(2 * pair + 2, steps - 1), 0)
        finish(2 * pair + 1, 1)
        return carry

    stats_ref[...] = jnp.zeros_like(stats_ref)
    put_scores(0, 0)
    lax.fori_loop(0, steps // 2, two_blocks, 0)
    copies += [started(locals_[i], outs[i], sems.at[i]) for i in (0, 1, 3)]
    for copy in copies:
        copy.wait()


def student_forward(place, inverse, heads, target, up, low):
    tokens = target.shape[0]
    one_pass = (1, *heads.shape[1:])
    smem = pl.BlockSpec(memory_space=pltpu.SMEM)
    outs = [
        jax.ShapeDtypeStruct((tokens, HDIM), BF),
        jax.ShapeDtypeStruct((tokens, HDIM), BF),
        jax.ShapeDtypeStruct((3, tokens, HDIM), BF),
        jax.ShapeDtypeStruct((8, tokens), F32),
    ]
    return pl.pallas_call(
        functools.partial(student_kernel, len(low)),
        grid=(1,),
        in_specs=[smem, smem, whole(one_pass)]
        + [whole(operand.shape) for operand in (target, up, *low)],
        out_specs=[HBM] * len(outs),
        out_shape=[pltpu.HBM(out.shape, out.dtype) for out in outs],
        scratch_shapes=[pltpu.VMEM(out.shape, out.dtype) for out in outs]
        + [
            pltpu.VMEM((HDIM, tokens), BF),
            pltpu.VMEM((tokens, 2 * HDIM), BF),
            pltpu.VMEM((2, 256, tokens), F32),
            pltpu.SemaphoreType.DMA((len(outs),)),
        ],
        cost_estimate=pl.CostEstimate(
            flops=4 * tokens * tokens * HDIM,
            transcendentals=tokens * tokens,
            bytes_accessed=6 * MIB,
        ),
        compiler_params=pltpu.CompilerParams(vmem_limit_bytes=48 * MIB),
        name="student_forward",
    )(place, inverse, heads, target, up, *low)


def backward_kernel(n_fast, place_ref, up_ref, *refs):
    n_in = n_fast + 3
    sources, outs, refs = refs[:n_in], refs[n_in : n_in + n_fast], refs[n_in + n_fast :]
    grad_up_ref, student_ref, upstream_ref, stats_ref, low_ref, back_ref = refs[:6]
    dq_ref, dk_ref, dv_ref, flat_ref, in_sems, out_sems = refs[6:]
    _, n_slow, rows, _ = low_ref.shape
    tokens = student_ref.shape[1]
    here_slow, here_fast = place_ref[0], place_ref[1]
    targets = [student_ref, upstream_ref, stats_ref] + [low_ref.at[d] for d in range(n_fast)]
    loads = [started(sources[i], targets[i], in_sems.at[i]) for i in range(n_in)]
    for load in loads[:3]:
        load.wait()
    step_rows = 512
    dk_ref[...] = jnp.zeros_like(dk_ref)
    dv_ref[...] = jnp.zeros_like(dv_ref)
    flat_ref[...] = jnp.transpose(student_ref[1])

    def one_block(step, carry):
        here = pl.ds(pl.multiple_of(step * step_rows, step_rows), step_rows)
        query = student_ref[0, here]
        upstream = upstream_ref[here]
        level = stats_ref[0:1, here]
        center = stats_ref[1:2, here]
        prob = jnp.exp2(dot(student_ref[1], query, NT) * SCALE2 - level)
        dv_ref[...] += dot(prob.astype(BF), upstream)
        dprob = dot(student_ref[2], upstream, NT)
        dscore = (prob * (dprob - center)).astype(BF)
        dk_ref[...] += dot(dscore, query)
        dq_ref[here] = jnp.transpose(dot(flat_ref[...], dscore))
        return carry

    lax.fori_loop(0, tokens // step_rows, one_block, 0)
    for load in loads[3:]:
        load.wait()

    def grads(ref, factor, slow, fast):
        block = lax.rem(here_slow + slow, n_slow) * n_fast + lax.rem(here_fast + fast, n_fast)
        grad = ref[pl.ds(pl.multiple_of(block * rows, rows), rows)] * factor
        return grad.astype(BF)

    parts = ((dq_ref, FACTOR), (dk_ref, FACTOR), (dv_ref, 1.0))
    stores = []
    for fast in (*range(1, n_fast), 0):
        for part, (ref, factor) in enumerate(parts):
            columns = slice(part * RANK, (part + 1) * RANK)
            for slow in range(n_slow):
                grad = grads(ref, factor, slow, fast)
                back_ref[fast, slow, :, columns] = dot(grad, up_ref[part], NT).astype(BF)
        stores.append(started(back_ref.at[fast], outs[fast], out_sems.at[fast]))
    for part, (ref, factor) in enumerate(parts):
        columns = slice(part * RANK, (part + 1) * RANK)
        total = jnp.zeros((RANK, HDIM), F32)
        for fast in range(n_fast):
            for slow in range(n_slow):
                grad = grads(ref, factor, n_slow - slow, n_fast - fast)
                total += dot(low_ref[fast, slow, :, columns], grad, TN)
        grad_up_ref[:, part * HDIM : (part + 1) * HDIM] = total.astype(BF)
    for store in stores:
        store.wait()


def backward(place, student, upstream, stats, up, low):
    tokens, n_fast = student.shape[1], len(low)
    up_shape = (RANK, 3 * HDIM)
    return pl.pallas_call(
        functools.partial(backward_kernel, n_fast),
        grid=(1,),
        in_specs=[pl.BlockSpec(memory_space=pltpu.SMEM), whole(up.shape)] + [HBM] * (n_fast + 3),
        out_specs=[HBM] * n_fast + [whole(up_shape)],
        out_shape=[pltpu.HBM(low[0].shape, BF)] * n_fast + [jax.ShapeDtypeStruct(up_shape, BF)],
        scratch_shapes=[
            pltpu.VMEM(student.shape, BF),
            pltpu.VMEM(upstream.shape, BF),
            pltpu.VMEM(stats.shape, F32),
            pltpu.VMEM((n_fast, *low[0].shape), BF),
            pltpu.VMEM((n_fast, *low[0].shape), BF),
            *[pltpu.VMEM((tokens, HDIM), F32)] * 3,
            pltpu.VMEM((HDIM, tokens), BF),
            pltpu.SemaphoreType.DMA((n_fast + 3,)),
            pltpu.SemaphoreType.DMA((n_fast,)),
        ],
        cost_estimate=pl.CostEstimate(
            flops=10 * tokens * tokens * HDIM,
            transcendentals=tokens * tokens,
            bytes_accessed=6 * MIB,
        ),
        compiler_params=pltpu.CompilerParams(vmem_limit_bytes=48 * MIB),
        name="attention_backward",
    )(place, up, *kept((student, upstream, stats, *low)))


def body(
    teacher_query,
    teacher_key,
    teacher_value,
    hidden,
    adapter_down_weight,
    adapter_up_weight,
    guidance_index,
    timestep_index,
):
    n_cfg, n_slow, n_fast = (lax.axis_size(a) for a in ("cfg", "z", "y"))
    n_x, n_core = (lax.axis_size(a) for a in ("x", "core"))
    cfg_index = lax.axis_index("cfg")
    seq_index = lax.axis_index(("z", "y"))
    features = hidden[0, 0]
    rows, width = features.shape
    tokens = rows * n_slow * n_fast
    total_rows = n_cfg * n_x * n_core * tokens

    packed = packed_by_head(teacher_query[0, :, 0], teacher_key[0, :, 0], teacher_value[0, :, 0])
    heads = exchange(packed, ("cfg", "z", "y"))
    heads = heads.reshape(n_cfg, n_slow * n_fast, 3, rows, HDIM)

    scale = 1.0 + 0.5 * lax.dynamic_slice(guidance_index[:, 0], (cfg_index,), (1,)).astype(F32)
    time = (lax.dynamic_slice(timestep_index[:, 0], (cfg_index,), (1,)).astype(F32) + 0.5) / TSTEPS
    rank_index = jnp.arange(1, RANK + 1).astype(F32)
    modulation = 1.0 + 0.5 * jnp.cos(math.pi * rank_index * time + 0.25 * rank_index * scale)

    low = [
        (dot(features, adapter_down_weight[part]) * modulation).astype(BF) for part in range(3)
    ]
    low = jnp.concatenate(low, axis=1)
    low_slow = jnp.stack(from_each(low, "z"))

    groups = n_cfg * n_slow
    part_cols = width // (groups * n_fast)
    spread = parts_ahead(features.reshape(rows, groups, n_fast, part_cols), "y", 2)
    spread = [part.reshape(rows, groups * part_cols) for part in spread]
    columns = [spread[0]] + [shifted(spread[d], "y", d) for d in range(1, n_fast - 1)]
    spread = spread[-1]

    place = jnp.stack([lax.axis_index("z"), lax.axis_index("y")]).astype(jnp.int32)
    up = lax.dynamic_slice_in_dim(adapter_up_weight, seq_index * HDIM, HDIM, 2)
    inverse = jnp.full((1,), 1.0 / math.sqrt(total_rows), F32)

    heads, low_slow, up, place, spread, *columns = lax.optimization_barrier(
        (heads, low_slow, up, place, spread, *columns)
    )
    low_all = from_each(low_slow, "y")
    target = teacher(scale, heads)
    target, *low_all = lax.optimization_barrier((target, *low_all))
    out, upstream, student, stats = student_forward(place, inverse, heads, target, up, low_all)
    tokens_out = exchange(out.reshape(n_slow * n_fast, rows, HDIM), ("z", "y"))

    *back, up_partial = backward(place, student, upstream, stats, up, low_all)
    tokens_out, up_partial, *back = lax.optimization_barrier((tokens_out, up_partial, *back))
    student_out = jnp.moveaxis(tokens_out, 0, 1).reshape(rows, -1)

    arrived = [shifted(back[d], "y", d) for d in range(1, n_fast)]
    arrived[0], spread = lax.optimization_barrier((arrived[0], spread))
    columns.append(shifted(spread, "y", n_fast - 1))
    back = sum((part.astype(F32) for part in arrived), back[0].astype(F32)).astype(BF)
    back, student_out = lax.optimization_barrier((back, student_out))
    back = summed_parts([back[d] for d in range(n_slow)], "z")
    low_grad = (back.reshape(rows, 3, RANK) * modulation).astype(BF).reshape(rows, 3 * RANK)
    low_grads = jnp.concatenate(from_each(low_grad, "y"))
    down = dot(jnp.concatenate(columns), low_grads, TN).astype(BF)
    down = down.reshape(n_cfg, n_slow, n_x, n_core, -1, 3 * RANK).transpose(3, 2, 0, 1, 4, 5)
    down_rows, up_rows = down.shape[-2], RANK // (n_cfg * n_x * n_core)
    down = down.reshape(n_core, n_x, n_cfg, n_slow * down_rows, 3 * RANK)
    up_partial = up_partial.reshape(n_cfg, n_x, n_core, up_rows, 3 * HDIM).transpose(2, 1, 0, 3, 4)
    both = reduced(jnp.concatenate([down, up_partial], axis=3), ("core", "x", "cfg"))
    down, grad_up = both[: n_slow * down_rows], both[n_slow * down_rows :]
    grad_up = jnp.moveaxis(grad_up.reshape(up_rows, 3, HDIM), 1, 0)
    down = reduced(down.reshape(n_slow, down_rows, 3 * RANK), ("z",))
    grad_down = jnp.moveaxis(down.reshape(down_rows, 3, RANK), 1, 0)
    return student_out[None, None], grad_down, grad_up


def solution(mesh):
    sizes = {"cfg": 2, "z": 4, "y": 4, "x": 4, "core": 2}
    mesh = Mesh(mesh.devices.reshape(tuple(sizes.values())), tuple(sizes))
    seq, dp = ("z", "y"), ("x", "core")
    teacher = P("cfg", None, dp, seq, None)
    return jax.shard_map(
        body,
        mesh=mesh,
        in_specs=(
            teacher,
            teacher,
            teacher,
            P("cfg", dp, seq, None),
            P(),
            P(),
            P(None, dp),
            P(None, dp),
        ),
        out_specs=(
            P("cfg", dp, seq, None),
            P(None, ("cfg", *seq, *dp), None),
            P(None, ("cfg", *dp), seq),
        ),
        check_vma=False,
    )
```

```python
import functools
import math

import jax
import jax.numpy as jnp
from jax import lax
from jax.experimental import pallas as pl
from jax.experimental.pallas import tpu as pltpu
from jax.sharding import Mesh
from jax.sharding import PartitionSpec as P

HDIM = 128
RANK = 128
TSTEPS = 1000
FACTOR = HDIM ** (-0.5)
LOG2E = math.log2(math.e)
SCALE2 = FACTOR * LOG2E
BF = jnp.bfloat16
F32 = jnp.float32
NT = (((1,), (1,)), ((), ()))
TN = (((0,), (0,)), ((), ()))
MIB = 1 << 20


def dot(a, b, dims=(((1,), (0,)), ((), ()))):
    return lax.dot_general(a, b, dims, preferred_element_type=F32)


def exchange(value, axes):
    return lax.all_to_all(value, axes, split_axis=0, concat_axis=0, tiled=True)


def shifted(value, axis, distance):
    size = lax.axis_size(axis)
    return lax.ppermute(value, axis, [(i, (i + distance) % size) for i in range(size)])


def from_each(value, axis):
    return [value] + [shifted(value, axis, d) for d in range(1, lax.axis_size(axis))]


def summed_parts(parts, axis):
    total = parts[0].astype(F32)
    for d in range(1, lax.axis_size(axis)):
        total = total + shifted(parts[d].astype(BF), axis, d).astype(F32)
    return total


def parts_ahead(value, axis, dim):
    size, here = lax.axis_size(axis), lax.axis_index(axis)
    return [
        lax.dynamic_index_in_dim(value, (here + d) % size, dim, keepdims=False)
        for d in range(size)
    ]


def reduced(value, axes):
    for axis in axes:
        value = summed_parts(parts_ahead(value, axis, 0), axis)
    return value


def whole(shape):
    return pl.BlockSpec(shape, lambda i: (0,) * len(shape))


HBM = pl.BlockSpec(memory_space=pltpu.HBM)


def kept(arrays):
    return [pltpu.with_memory_space_constraint(array, pltpu.HBM) for array in arrays]


def started(source, target, semaphore):
    copy = pltpu.make_async_copy(source, target, semaphore)
    copy.start()
    return copy


def pack_kernel(q_ref, k_ref, v_ref, out_ref):
    heads = out_ref.shape[0]
    for part, ref in enumerate((q_ref, k_ref, v_ref)):
        for head in range(heads):
            out_ref[head, part] = ref[0, :, head * HDIM : (head + 1) * HDIM]


def packed_by_head(q, k, v):
    halves, rows, columns = q.shape
    heads = columns // HDIM
    spec = pl.BlockSpec((1, rows, columns), lambda i: (i, 0, 0))
    return pl.pallas_call(
        pack_kernel,
        grid=(halves,),
        in_specs=[spec] * 3,
        out_specs=pl.BlockSpec((heads, 3, rows, HDIM), lambda i: (i, 0, 0, 0)),
        out_shape=jax.ShapeDtypeStruct((halves * heads, 3, rows, HDIM), q.dtype),
        cost_estimate=pl.CostEstimate(flops=0, transcendentals=0, bytes_accessed=12 * q.size),
        name="pack_heads",
    )(q, k, v)


def with_ones(ref, values):
    ref[:, :HDIM] = values
    ref[:, HDIM:] = jnp.ones_like(values)


def attended_rows(scores, value_ref):
    highest = jnp.max(scores, axis=-1, keepdims=True)
    raised = jnp.exp2((scores - highest) * SCALE2).astype(BF)
    both = dot(raised, value_ref[...])
    total = both[:, HDIM:]
    return both[:, :HDIM] / total, highest, total


def teacher_kernel(heads_ref, out_ref, query_ref, key_ref, value_ref, scores_ref):
    blocks, rows = heads_ref.shape[1], heads_ref.shape[3]
    for block in range(blocks):
        where = slice(block * rows, (block + 1) * rows)
        query_ref[where] = heads_ref[0, block, 0]
        key_ref[:, where] = jnp.transpose(heads_ref[0, block, 1])
        with_ones(value_ref.at[where], heads_ref[0, block, 2])
    step_rows = scores_ref.shape[1]
    steps = blocks * rows // step_rows

    def rows_of(step):
        return pl.ds(pl.multiple_of(step * step_rows, step_rows), step_rows)

    def put_scores(step, slot):
        scores_ref[slot] = dot(query_ref[rows_of(step)], key_ref[...])

    def finish(step, slot):
        out_ref[rows_of(step)] = attended_rows(scores_ref[slot], value_ref)[0].astype(BF)

    def two_blocks(pair, carry):
        put_scores(2 * pair + 1, 1)
        finish(2 * pair, 0)
        put_scores(jnp.minimum(2 * pair + 2, steps - 1), 0)
        finish(2 * pair + 1, 1)
        return carry

    put_scores(0, 0)
    lax.fori_loop(0, steps // 2, two_blocks, 0)


def teacher(heads, one):
    tokens = heads.shape[1] * heads.shape[3]
    return pl.pallas_call(
        teacher_kernel,
        grid=(1,),
        in_specs=[pl.BlockSpec((1, *heads.shape[1:]), lambda i: (one, 0, 0, 0, 0))],
        out_specs=whole((tokens, HDIM)),
        out_shape=jax.ShapeDtypeStruct((tokens, HDIM), BF),
        scratch_shapes=[
            pltpu.VMEM((tokens, HDIM), BF),
            pltpu.VMEM((HDIM, tokens), BF),
            pltpu.VMEM((tokens, 2 * HDIM), BF),
            pltpu.VMEM((2, 256, tokens), F32),
        ],
        cost_estimate=pl.CostEstimate(
            flops=4 * tokens * tokens * HDIM,
            transcendentals=tokens * tokens,
            bytes_accessed=2 * MIB,
        ),
        compiler_params=pltpu.CompilerParams(vmem_limit_bytes=48 * MIB),
        name="teacher_forward",
    )(heads)


def student_kernel(n_fast, place_ref, scale_ref, inv_ref, heads_ref, *refs):
    cond_ref, uncond_ref, up_ref, *refs = refs
    low_refs = refs[:n_fast]
    outs, locals_ = refs[n_fast : n_fast + 4], refs[n_fast + 4 : n_fast + 8]
    out_ref, upstream_ref, student_ref, stats_ref = locals_
    key_ref, value_ref, scores_ref, sems = refs[n_fast + 8 :]
    rows = heads_ref.shape[3]
    tokens = out_ref.shape[0]
    n_slow = low_refs[0].shape[0]
    here_slow, here_fast = place_ref[0], place_ref[1]
    scale, inverse = scale_ref[0], inv_ref[0]

    for part in range(3):
        up = up_ref[part]
        for fast in range(n_fast):
            low = low_refs[fast][:, :, part * RANK : (part + 1) * RANK]
            adapted = dot(low.reshape(n_slow * rows, RANK), up)
            for slow in range(n_slow):
                block = lax.rem(here_slow - slow + n_slow, n_slow) * n_fast + lax.rem(
                    here_fast - fast + n_fast, n_fast
                )
                frozen = heads_ref[0, block, part].astype(F32)
                where = pl.ds(pl.multiple_of(block * rows, rows), rows)
                student_ref[part, where] = (
                    frozen + adapted[slow * rows : (slow + 1) * rows]
                ).astype(BF)
    copies = [started(student_ref, outs[2], sems.at[2])]
    for block in range(n_slow * n_fast):
        where = slice(block * rows, (block + 1) * rows)
        key_ref[:, where] = jnp.transpose(student_ref[1, where])
        with_ones(value_ref.at[where], student_ref[2, where])
    step_rows = scores_ref.shape[1]
    steps = tokens // step_rows

    def rows_of(step):
        return pl.ds(pl.multiple_of(step * step_rows, step_rows), step_rows)

    def put_scores(step, slot):
        scores_ref[slot] = dot(student_ref[0, rows_of(step)], key_ref[...])

    def finish(step, slot):
        here = rows_of(step)
        attended, highest, total = attended_rows(scores_ref[slot], value_ref)
        rounded = attended.astype(BF)
        out_ref[here] = rounded
        unconditional = uncond_ref[here].astype(F32)
        target = unconditional + scale * (cond_ref[here].astype(F32) - unconditional)
        upstream = ((rounded.astype(F32) - target) * inverse).astype(BF)
        upstream_ref[here] = upstream
        level = highest * SCALE2 + jnp.log2(total)
        center = jnp.sum(attended * upstream.astype(F32), axis=-1, keepdims=True)
        stats_ref[0:1, here] = jnp.transpose(level)[0:1]
        stats_ref[1:2, here] = jnp.transpose(jnp.broadcast_to(center, (step_rows, HDIM)))[0:1]

    def two_blocks(pair, carry):
        put_scores(2 * pair + 1, 1)
        finish(2 * pair, 0)
        put_scores(jnp.minimum(2 * pair + 2, steps - 1), 0)
        finish(2 * pair + 1, 1)
        return carry

    stats_ref[...] = jnp.zeros_like(stats_ref)
    put_scores(0, 0)
    lax.fori_loop(0, steps // 2, two_blocks, 0)
    copies += [started(locals_[i], outs[i], sems.at[i]) for i in (0, 1, 3)]
    for copy in copies:
        copy.wait()


def student_forward(place, scale, inverse, heads, teachers, up, low):
    tokens = teachers[0].shape[0]
    one_pass = (1, *heads.shape[1:])
    smem = pl.BlockSpec(memory_space=pltpu.SMEM)
    outs = [
        jax.ShapeDtypeStruct((tokens, HDIM), BF),
        jax.ShapeDtypeStruct((tokens, HDIM), BF),
        jax.ShapeDtypeStruct((3, tokens, HDIM), BF),
        jax.ShapeDtypeStruct((8, tokens), F32),
    ]
    return pl.pallas_call(
        functools.partial(student_kernel, len(low)),
        grid=(1,),
        in_specs=[smem, smem, smem, whole(one_pass)]
        + [whole(operand.shape) for operand in (*teachers, up, *low)],
        out_specs=[HBM] * len(outs),
        out_shape=[pltpu.HBM(out.shape, out.dtype) for out in outs],
        scratch_shapes=[pltpu.VMEM(out.shape, out.dtype) for out in outs]
        + [
            pltpu.VMEM((HDIM, tokens), BF),
            pltpu.VMEM((tokens, 2 * HDIM), BF),
            pltpu.VMEM((2, 256, tokens), F32),
            pltpu.SemaphoreType.DMA((len(outs),)),
        ],
        cost_estimate=pl.CostEstimate(
            flops=4 * tokens * tokens * HDIM,
            transcendentals=tokens * tokens,
            bytes_accessed=6 * MIB,
        ),
        compiler_params=pltpu.CompilerParams(vmem_limit_bytes=48 * MIB),
        name="student_forward",
    )(place, scale, inverse, heads, *teachers, up, *low)


def backward_kernel(n_fast, place_ref, up_ref, *refs):
    n_in = n_fast + 3
    sources, outs, refs = refs[:n_in], refs[n_in : n_in + n_fast], refs[n_in + n_fast :]
    grad_up_ref, student_ref, upstream_ref, stats_ref, low_ref, back_ref = refs[:6]
    dq_ref, dk_ref, dv_ref, flat_ref, in_sems, out_sems = refs[6:]
    _, n_slow, rows, _ = low_ref.shape
    tokens = student_ref.shape[1]
    here_slow, here_fast = place_ref[0], place_ref[1]
    targets = [student_ref, upstream_ref, stats_ref] + [low_ref.at[d] for d in range(n_fast)]
    loads = [started(sources[i], targets[i], in_sems.at[i]) for i in range(n_in)]
    for load in loads[:3]:
        load.wait()
    step_rows = 512
    dk_ref[...] = jnp.zeros_like(dk_ref)
    dv_ref[...] = jnp.zeros_like(dv_ref)
    flat_ref[...] = jnp.transpose(student_ref[1])

    def one_block(step, carry):
        here = pl.ds(pl.multiple_of(step * step_rows, step_rows), step_rows)
        query = student_ref[0, here]
        upstream = upstream_ref[here]
        level = stats_ref[0:1, here]
        center = stats_ref[1:2, here]
        prob = jnp.exp2(dot(student_ref[1], query, NT) * SCALE2 - level)
        dv_ref[...] += dot(prob.astype(BF), upstream)
        dprob = dot(student_ref[2], upstream, NT)
        dscore = (prob * (dprob - center)).astype(BF)
        dk_ref[...] += dot(dscore, query)
        dq_ref[here] = jnp.transpose(dot(flat_ref[...], dscore))
        return carry

    lax.fori_loop(0, tokens // step_rows, one_block, 0)
    for load in loads[3:]:
        load.wait()

    def grads(ref, factor, slow, fast):
        block = lax.rem(here_slow + slow, n_slow) * n_fast + lax.rem(here_fast + fast, n_fast)
        grad = ref[pl.ds(pl.multiple_of(block * rows, rows), rows)] * factor
        return grad.astype(BF)

    parts = ((dq_ref, FACTOR), (dk_ref, FACTOR), (dv_ref, 1.0))
    stores = []
    for fast in (*range(1, n_fast), 0):
        for part, (ref, factor) in enumerate(parts):
            columns = slice(part * RANK, (part + 1) * RANK)
            for slow in range(n_slow):
                grad = grads(ref, factor, slow, fast)
                back_ref[fast, slow, :, columns] = dot(grad, up_ref[part], NT).astype(BF)
        stores.append(started(back_ref.at[fast], outs[fast], out_sems.at[fast]))
    for part, (ref, factor) in enumerate(parts):
        columns = slice(part * RANK, (part + 1) * RANK)
        total = jnp.zeros((RANK, HDIM), F32)
        for fast in range(n_fast):
            for slow in range(n_slow):
                grad = grads(ref, factor, n_slow - slow, n_fast - fast)
                total += dot(low_ref[fast, slow, :, columns], grad, TN)
        grad_up_ref[:, part * HDIM : (part + 1) * HDIM] = total.astype(BF)
    for store in stores:
        store.wait()


def backward(place, student, upstream, stats, up, low):
    tokens, n_fast = student.shape[1], len(low)
    up_shape = (RANK, 3 * HDIM)
    return pl.pallas_call(
        functools.partial(backward_kernel, n_fast),
        grid=(1,),
        in_specs=[pl.BlockSpec(memory_space=pltpu.SMEM), whole(up.shape)] + [HBM] * (n_fast + 3),
        out_specs=[HBM] * n_fast + [whole(up_shape)],
        out_shape=[pltpu.HBM(low[0].shape, BF)] * n_fast + [jax.ShapeDtypeStruct(up_shape, BF)],
        scratch_shapes=[
            pltpu.VMEM(student.shape, BF),
            pltpu.VMEM(upstream.shape, BF),
            pltpu.VMEM(stats.shape, F32),
            pltpu.VMEM((n_fast, *low[0].shape), BF),
            pltpu.VMEM((n_fast, *low[0].shape), BF),
            *[pltpu.VMEM((tokens, HDIM), F32)] * 3,
            pltpu.VMEM((HDIM, tokens), BF),
            pltpu.SemaphoreType.DMA((n_fast + 3,)),
            pltpu.SemaphoreType.DMA((n_fast,)),
        ],
        cost_estimate=pl.CostEstimate(
            flops=10 * tokens * tokens * HDIM,
            transcendentals=tokens * tokens,
            bytes_accessed=6 * MIB,
        ),
        compiler_params=pltpu.CompilerParams(vmem_limit_bytes=48 * MIB),
        name="attention_backward",
    )(place, up, *kept((student, upstream, stats, *low)))


def body(
    teacher_query,
    teacher_key,
    teacher_value,
    hidden,
    adapter_down_weight,
    adapter_up_weight,
    guidance_index,
    timestep_index,
):
    n_cfg, n_slow, n_fast = (lax.axis_size(a) for a in ("cfg", "z", "y"))
    n_x, n_core = (lax.axis_size(a) for a in ("x", "core"))
    cfg_index = lax.axis_index("cfg")
    seq_index = lax.axis_index(("z", "y"))
    features = hidden[0, 0]
    rows, width = features.shape
    tokens = rows * n_slow * n_fast
    total_rows = n_cfg * n_x * n_core * tokens

    packed = packed_by_head(teacher_query[0, :, 0], teacher_key[0, :, 0], teacher_value[0, :, 0])
    heads = exchange(packed, ("cfg", "z", "y"))
    heads = heads.reshape(n_cfg, n_slow * n_fast, 3, rows, HDIM)

    scale = 1.0 + 0.5 * lax.dynamic_slice(guidance_index[:, 0], (cfg_index,), (1,)).astype(F32)
    time = (lax.dynamic_slice(timestep_index[:, 0], (cfg_index,), (1,)).astype(F32) + 0.5) / TSTEPS
    rank_index = jnp.arange(1, RANK + 1).astype(F32)
    modulation = 1.0 + 0.5 * jnp.cos(math.pi * rank_index * time + 0.25 * rank_index * scale)

    low = [
        (dot(features, adapter_down_weight[part]) * modulation).astype(BF) for part in range(3)
    ]
    low = jnp.concatenate(low, axis=1)
    groups = n_cfg * n_slow
    part_cols = width // (groups * n_fast)
    spread = parts_ahead(features.reshape(rows, groups, n_fast, part_cols), "y", 2)
    spread = [part.reshape(rows, groups * part_cols) for part in spread]
    columns = [spread[0]] + [shifted(spread[d], "y", d) for d in range(1, n_fast)]

    place = jnp.stack([lax.axis_index("z"), lax.axis_index("y")]).astype(jnp.int32)
    up = lax.dynamic_slice_in_dim(adapter_up_weight, seq_index * HDIM, HDIM, 2)
    inverse = jnp.full((1,), 1.0 / math.sqrt(total_rows), F32)

    heads, low, up, place, *columns = lax.optimization_barrier((heads, low, up, place, *columns))
    low_slow = from_each(low, "z")
    conditional = teacher(heads, 0)
    conditional, heads, *low_slow = lax.optimization_barrier((conditional, heads, *low_slow))
    low_all = from_each(jnp.stack(low_slow), "y")
    unconditional = teacher(heads, 1)
    unconditional, *low_all = lax.optimization_barrier((unconditional, *low_all))
    teachers = (conditional, unconditional)
    out, upstream, student, stats = student_forward(
        place, scale.reshape(1), inverse, heads, teachers, up, low_all
    )
    tokens_out = exchange(out.reshape(n_slow * n_fast, rows, HDIM), ("z", "y"))

    *back, up_partial = backward(place, student, upstream, stats, up, low_all)
    tokens_out, up_partial, *back = lax.optimization_barrier((tokens_out, up_partial, *back))
    student_out = jnp.moveaxis(tokens_out, 0, 1).reshape(rows, -1)

    arrived = [shifted(back[d], "y", d) for d in range(1, n_fast)]
    back = sum((part.astype(F32) for part in arrived), back[0].astype(F32)).astype(BF)
    back, student_out = lax.optimization_barrier((back, student_out))
    back = summed_parts([back[d] for d in range(n_slow)], "z")
    low_grad = (back.reshape(rows, 3, RANK) * modulation).astype(BF).reshape(rows, 3 * RANK)
    low_grads = jnp.concatenate(from_each(low_grad, "y"))
    down = dot(jnp.concatenate(columns), low_grads, TN).astype(BF)
    down = down.reshape(n_cfg, n_slow, n_x, n_core, -1, 3 * RANK).transpose(3, 2, 0, 1, 4, 5)
    down_rows, up_rows = down.shape[-2], RANK // (n_cfg * n_x * n_core)
    down = down.reshape(n_core, n_x, n_cfg, n_slow * down_rows, 3 * RANK)
    up_partial = up_partial.reshape(n_cfg, n_x, n_core, up_rows, 3 * HDIM).transpose(2, 1, 0, 3, 4)
    both = reduced(jnp.concatenate([down, up_partial], axis=3), ("core", "x", "cfg"))
    down, grad_up = both[: n_slow * down_rows], both[n_slow * down_rows :]
    grad_up = jnp.moveaxis(grad_up.reshape(up_rows, 3, HDIM), 1, 0)
    down = reduced(down.reshape(n_slow, down_rows, 3 * RANK), ("z",))
    grad_down = jnp.moveaxis(down.reshape(down_rows, 3, RANK), 1, 0)
    return student_out[None, None], grad_down, grad_up


def solution(mesh):
    sizes = {"cfg": 2, "z": 4, "y": 4, "x": 4, "core": 2}
    mesh = Mesh(mesh.devices.reshape(tuple(sizes.values())), tuple(sizes))
    seq, dp = ("z", "y"), ("x", "core")
    teacher = P("cfg", None, dp, seq, None)
    return jax.shard_map(
        body,
        mesh=mesh,
        in_specs=(
            teacher,
            teacher,
            teacher,
            P("cfg", dp, seq, None),
            P(),
            P(),
            P(None, dp),
            P(None, dp),
        ),
        out_specs=(
            P("cfg", dp, seq, None),
            P(None, ("cfg", *seq, *dp), None),
            P(None, ("cfg", *dp), seq),
        ),
        check_vma=False,
    )
```
